32 devices in a mesh: group: 2 (over x), seq: 16 (over z, y, core).
Axes of the slice: x: 2, y: 2, z: 4, core: 2. Of those that a mesh axis runs over, the one named last changes fastest.
Arguments:
- inputs: float32 [16384, 2560], P(('group', 'seq')), parts along dimension 0, may hold values from -6 to 6
- log_decay: float32 [40, 16384], P(None, ('group', 'seq')), parts along dimension 1, may hold values from -0.8 to 0, as said below
- state_write: float32 [16384, 128], P(('group', 'seq')), parts along dimension 0, may hold values from -0.5 to 0.5
- state_read: float32 [16384, 128], P(('group', 'seq')), parts along dimension 0, may hold values from -0.5 to 0.5
- skip_gain: float32 [40], replicated, may hold values from 0.5 to 1.5
- grad_output: float32 [16384, 2560], P(('group', 'seq')), parts along dimension 0, may hold values from -6 to 6
Outputs:
- outputs: float32 [16384, 2560], P(('group', 'seq')), parts along dimension 0
- grad_inputs: float32 [16384, 2560], P(('group', 'seq')), parts along dimension 0
- grad_decay: float32 [40, 16384], P(None, ('group', 'seq')), parts along dimension 1
- grad_write: float32 [16384, 128], P(('group', 'seq')), parts along dimension 0
- grad_read: float32 [16384, 128], P(('group', 'seq')), parts along dimension 0
The draws below stay inside these ranges and needn't reach their ends.
There are 2 independent parts, one for each index of `group`. The reference program is written for one: setup_inputs(seed, part) draws one part's arguments, and reference() takes and returns one part's arrays. A program takes and returns all parts, laid end to end along the dimension named above; an argument that names none is the same for every part. Nothing has to cross between parts.
Inputs may be any that keep to these rules, and one draw needn't show every extreme that they name: `log_decay`: log retention of each head at each position; never positive.
All inputs are finite; a program needn't handle non-finite values.
Results may differ from the reference program's by a relative error of at most 0.00021.
Values sent between devices are 32-bit elements; how exact they have to be, the bound alone decides.
No kernel may reach another device: no remote copies, remote signals or barrier semaphores. Data moves between devices by JAX's collectives and lax.ppermute only.
A program may use at most 256 MiB of HBM per device.

```python
import jax
import jax.numpy as jnp
from jax import lax

H = 40
P_SIZE = 64
N = 128
BLOCK = 256
TOK_DEV = 512
TOKENS = 8192


def draw_log_decay(key, part):
    keys = jax.random.split(key, 7)
    share = 0.5
    fast_heads = jax.random.uniform(keys[0], (H,)) < share
    fast_rate = jax.random.uniform(keys[1], (H,), jnp.float32, 1.0 / 50.0, 1.0 / 30.0)
    slow_rate = 0.4 / TOKENS * jax.random.uniform(keys[2], (H,), jnp.float32, 0.5, 1.0)
    baseline_decay_rate = jnp.where(fast_heads, fast_rate, slow_rate)
    device_factor = jax.random.uniform(keys[3], (TOKENS // TOK_DEV,), jnp.float32, 0.35, 1.0)
    position_factor = jnp.repeat(device_factor, TOK_DEV)
    rough = jax.random.uniform(keys[4], (H, TOKENS), jnp.float32, 0.5, 1.5)
    decay_rate = baseline_decay_rate[:, None] * position_factor[None, :] * rough
    spike_locations = jax.random.randint(keys[5], (2,), 0, TOKENS)
    loss_values = jax.random.uniform(keys[6], (2, H), jnp.float32, 0.2, 0.5)
    device_positions = jnp.arange(TOKENS)
    spike_amplitude = jnp.where(device_positions[None, :] == spike_locations[0], jnp.log(1.0 - loss_values[0])[:, None], 0.0)
    spike_amplitude = spike_amplitude + jnp.where(device_positions[None, :] == spike_locations[1], jnp.log(1.0 - loss_values[1])[:, None], 0.0)
    return (spike_amplitude - decay_rate).astype(jnp.float32)


def steps_of(rng, extent, cuts, low, largest):
    def one(axis_at, parts):
        draws = jax.random.uniform(jax.random.fold_in(jax.random.fold_in(rng, 6), axis_at), (parts,), jnp.float32, low / len(cuts), largest / len(cuts))
        return jnp.repeat(jnp.exp(draws), extent[axis_at] // parts).reshape((-1,) + (1,) * (len(extent) - axis_at - 1))

    gain = one(*cuts[0])
    for cut in cuts[1:]:
        gain = gain * one(*cut)
    return gain


def gaussian(key, shape, spread, bound, cuts=(), kind=jnp.bfloat16):
    gain = steps_of(key, shape, cuts, -0.22, 0.18) if cuts else 1.0
    entries = jax.random.normal(key, shape, jnp.float32) * spread * gain
    return jnp.minimum(jnp.maximum(entries, -bound), bound).astype(kind)


def setup_inputs(seed: int = 0, part: int = 0) -> dict:
    key_of = jax.random.split(jax.random.key(seed), 7)
    part_keys = jax.random.split(jax.random.fold_in(key_of[6], part), 7)
    return {
        "inputs": gaussian(part_keys[0], (TOKENS, H * P_SIZE), 1.0, 6.0, ((0, 16),), jnp.float32),
        "log_decay": draw_log_decay(jax.random.fold_in(jax.random.fold_in(key_of[6], part), 71), part),
        "state_write": gaussian(part_keys[2], (TOKENS, N), ((N * TOKENS) ** -0.25), 0.5, ((0, 16),), jnp.float32),
        "state_read": gaussian(part_keys[3], (TOKENS, N), ((N * TOKENS) ** -0.25), 0.5, ((0, 16),), jnp.float32),
        "skip_gain": jnp.clip(1.0 + 0.1 * jax.random.normal(key_of[4], (H,), jnp.float32), 0.5, 1.5),
        "grad_output": gaussian(part_keys[5], (TOKENS, H * P_SIZE), 1.0, 6.0, ((0, 16),), jnp.float32),
    }


def block_pass(inputs, log_decay, state_write, state_read, skip_gain, start_state):
    tok_rows = inputs.shape[0]
    head_count = log_decay.shape[0]
    head_width = inputs.shape[1] // head_count
    block_count = tok_rows // BLOCK
    shaped = inputs.reshape(block_count, BLOCK, head_count, head_width)
    decays = log_decay.reshape(head_count, block_count, BLOCK).transpose(1, 0, 2)
    writes = state_write.reshape(block_count, BLOCK, -1)
    reads = state_read.reshape(block_count, BLOCK, -1)
    lower_mask = jnp.arange(BLOCK)[:, None] >= jnp.arange(BLOCK)[None, :]

    def advance(carried_state, pieces):
        values, decay_block, write_block, read_block = pieces
        cum_decay = jnp.cumsum(decay_block, axis=1)
        intersection = jnp.dot(read_block, write_block.T, precision=lax.Precision.HIGHEST)
        gap_decay = jnp.where(lower_mask[None], cum_decay[:, :, None] - cum_decay[:, None, :], 0.0)
        mixing = jnp.where(lower_mask[None], jnp.exp(gap_decay), 0.0) * intersection[None]
        inner_part = jnp.einsum('hts,shp->thp', mixing, values, precision=lax.Precision.HIGHEST)
        carried_portion = jnp.einsum('tn,hpn->thp', read_block, carried_state, precision=lax.Precision.HIGHEST)
        carried_portion = carried_portion * jnp.exp(cum_decay).T[:, :, None]
        tail_weight = jnp.exp(cum_decay[:, -1:] - cum_decay).T
        update = jnp.einsum('shp,sn->hpn', values * tail_weight[:, :, None], write_block, precision=lax.Precision.HIGHEST)
        next_state = jnp.exp(cum_decay[:, -1])[:, None, None] * carried_state + update
        emitted = inner_part + carried_portion + skip_gain[None, :, None] * values
        return (next_state, emitted.reshape(BLOCK, head_count * head_width))
    final_state, emitted = lax.scan(jax.checkpoint(advance), start_state, (shaped, decays, writes, reads))
    return (emitted.reshape(tok_rows, head_count * head_width), final_state)

def reference(inputs, log_decay, state_write, state_read, skip_gain, grad_output):
    start_state = jnp.zeros((H, P_SIZE, N), jnp.float32)

    def local_fn(values, decay_rows, write_rows, read_rows):
        return block_pass(values, decay_rows, write_rows, read_rows, skip_gain, start_state)
    (outputs, final_state), pullback = jax.vjp(local_fn, inputs, log_decay, state_write, state_read)
    grad_inputs, grad_decay, grad_write, grad_read = pullback((grad_output, jnp.zeros_like(final_state)))
    return (outputs, grad_inputs, grad_decay, grad_write, grad_read)
```

```python
import functools

import jax
import jax.numpy as jnp
from jax import lax
from jax.experimental import pallas as pl
from jax.experimental.pallas import tpu as pltpu
from jax.sharding import PartitionSpec as P

CHUNK = 128
LANES = 512
GROUPS = (3, 2)
F32 = jnp.float32
BF16 = jnp.bfloat16


def dot(a, b):
    return lax.dot_general(a, b, (((1,), (0,)), ((), ())), preferred_element_type=F32)


def dot_nt(a, b):
    return lax.dot_general(a, b, (((1,), (1,)), ((), ())), preferred_element_type=F32)


def split(x):
    high = x.astype(BF16)
    return high, (x - high.astype(F32)).astype(BF16)


def split3(x):
    high = x.astype(BF16)
    rest = x - high.astype(F32)
    middle = rest.astype(BF16)
    return high, middle, (rest - middle.astype(F32)).astype(BF16)


def three(product, a, b):
    return product(a[0], b[0]) + product(a[0], b[1]) + product(a[1], b[0])


def iota(shape, axis):
    return lax.broadcasted_iota(jnp.int32, shape, axis)


def fold3(x, heads):
    high, middle, low = split3(x)
    column = iota(x.shape, 1)
    chosen = jnp.where(
        column < heads,
        high.astype(F32),
        jnp.where(column < 2 * heads, middle.astype(F32), low.astype(F32)),
    )
    return chosen.astype(BF16)


def spread_matrix(rows, lanes, first, heads, width):
    row, lane = iota((rows, lanes), 0), iota((rows, lanes), 1)
    hit = None
    for copy in range(3):
        start = (row - (first + copy * heads)) * width
        one = jnp.logical_and(lane >= start, lane < start + width)
        hit = one if hit is None else jnp.logical_or(hit, one)
    return jnp.where(hit, 1.0, 0.0).astype(BF16)


def pack_decay(packed, decay_ref, heads):
    packed[...] = jnp.zeros_like(packed)
    for copy in range(3):
        packed[copy * heads : (copy + 1) * heads, :] = decay_ref[...]


def state_kernel(
    slot_ref, decay_ref, write_ref, read_ref, x_ref, g_ref, keep_ref, send_ref,
    packed, tail, lead, write_t, read_t, stage, *, first_head, heads, width
):
    step = pl.program_id(0)
    rows, lanes = x_ref.shape
    state = write_ref.shape[1]
    quarter = state // 4

    @pl.when(step == 0)
    def _():
        pack_decay(packed, decay_ref, heads)
        parts = split3(packed[...])
        t, u = iota((rows, rows), 0), iota((rows, rows), 1)
        before = jnp.where(u <= t, 1.0, 0.0).astype(BF16)
        after = jnp.where(u > t, 1.0, 0.0).astype(BF16)
        lead[...] = fold3(jnp.exp(sum(dot_nt(before, p) for p in parts)), heads)
        tail[...] = fold3(jnp.exp(sum(dot_nt(after, p) for p in parts)), heads)
        write_t[0], write_t[1] = split(write_ref[...].T)
        read_t[0], read_t[1] = split(read_ref[...].T)

    first = first_head + step * (lanes // width)
    spread = spread_matrix(packed.shape[0], lanes, first, heads, width)
    slot = slot_ref[0]
    for which, (value_ref, weight, factor) in enumerate(
        ((x_ref, tail, write_t), (g_ref, lead, read_t))
    ):
        scaled = split(value_ref[...] * dot(weight[...], spread))
        stage[which] = three(dot, (factor[0], factor[1]), scaled)
        for relative in range(4):
            start = pl.multiple_of((slot ^ relative) * quarter, quarter)
            target = keep_ref if relative < 2 else send_ref
            target[which, relative % 2] = stage[which, pl.ds(start, quarter), :]


def block_kernel(
    slot_ref, decay_ref, write_ref, read_ref, skip_ref, x_ref, g_ref, mine_ref, other_ref,
    *refs, first_head, heads, width, chained
):
    if chained:
        _, _, old_decay, old_write, old_read, *refs = refs
    (
        y_ref, dx_ref, gd_ref, gw_ref, gr_ref,
        packed, up, down, edges, left_y, left_x, write_t, read_t,
        row_sums, acc_read, acc_write, state_in, grad_in, ups, downs, right_h, right_l, held, inner
    ) = refs
    step, last = pl.program_id(0), pl.num_programs(0) - 1
    rows, lanes = x_ref.shape
    state = write_ref.shape[1]
    quarter = state // 4
    count = rows // CHUNK
    middle = CHUNK // 2 - 1
    span = [slice(i * CHUNK, (i + 1) * CHUNK) for i in range(count)]

    @pl.when(step == 0)
    def _():
        pack_decay(packed, decay_ref, heads)
        t, u = iota((CHUNK, CHUNK), 0), iota((CHUNK, CHUNK), 1)
        ahead = jnp.logical_and(u > middle, u <= t)
        behind = jnp.logical_and(u <= middle, u > t)
        signed = jnp.where(ahead, 1.0, jnp.where(behind, -1.0, 0.0)).astype(BF16)
        row, column = iota((16, CHUNK), 0), iota((16, CHUNK), 1)
        half = jnp.where((row == 0) == (column <= middle), 1.0, 0.0).astype(BF16)
        for i in range(count):
            parts = split3(packed[:, span[i]])
            gap = sum(dot_nt(signed, p) for p in parts)
            up[span[i], :] = fold3(jnp.exp(gap), heads)
            down[span[i], :] = fold3(jnp.exp(-gap), heads)
            edges[i] = fold3(jnp.exp(sum(dot_nt(half, p) for p in parts)), heads)
            write, read = write_ref[span[i], :], read_ref[span[i], :]
            write_p, read_p = split(write), split(read)
            scores = jnp.where(u <= t, three(dot_nt, read_p, write_p), 0.0)
            left_y[0, i], left_y[1, i] = split(jnp.concatenate([scores, read], 1))
            scores = jnp.where(u >= t, three(dot_nt, write_p, read_p), 0.0)
            left_x[0, i], left_x[1, i] = split(jnp.concatenate([scores, write], 1))
            write_t[i] = jnp.concatenate(split(write.T), 1)
            read_t[i] = jnp.concatenate(split(read.T), 1)
        row_sums[...] = jnp.zeros_like(row_sums)
        acc_read[...] = jnp.zeros_like(acc_read)
        acc_write[...] = jnp.zeros_like(acc_write)

    first = first_head + step * (lanes // width)
    spread = spread_matrix(packed.shape[0], lanes, first, heads, width)
    ups[...] = dot(up[...], spread)
    downs[...] = dot(down[...], spread)
    edge = [dot(edges[i], spread) for i in range(count)]
    skip = skip_ref[...]
    slot = slot_ref[0]
    for relative in range(4):
        start = pl.multiple_of((slot ^ relative) * quarter, quarter)
        source = mine_ref if relative < 2 else other_ref
        state_in[pl.ds(start, quarter), :] = source[0, relative % 2]
        grad_in[pl.ds(start, quarter), :] = source[1, relative % 2]

    carried = edge[0][0:1] * state_in[...]
    for i in range(count):
        x = x_ref[span[i], :]
        xh, xl = split(x * downs[span[i], :])
        ph, pl_ = split(carried)
        right_h[i] = jnp.concatenate([xh, ph], 0)
        right_l[i] = jnp.concatenate([xl, pl_], 0)
        made = three(dot, (left_y[0, i], left_y[1, i]), (right_h[i], right_l[i]))
        made = made * ups[span[i], :]
        y_ref[span[i], :] = made + skip * x
        inner[span[i], :] = made * g_ref[span[i], :]
        gained = dot(write_t[i], jnp.concatenate([xh, xh], 0)) + dot(write_t[i, :, :CHUNK], xl)
        total = carried + gained
        held[i] = total
        if i + 1 < count:
            carried = edge[i + 1][0:1] * (edge[i][1:2] * total)

    row, lane = iota((lanes, packed.shape[0]), 0), iota((lanes, packed.shape[0]), 1)
    begin = (lane - first) * width
    gather = jnp.where(jnp.logical_and(row >= begin, row < begin + width), 1.0, 0.0).astype(BF16)
    bottom = iota((CHUNK, 1), 0) == CHUNK - 1
    carried = edge[count - 1][1:2] * grad_in[...]
    for i in reversed(range(count)):
        g = g_ref[span[i], :]
        x = x_ref[span[i], :]
        gh, gl = split(g * ups[span[i], :])
        qh, ql = split(carried)
        right = (jnp.concatenate([gh, qh], 0), jnp.concatenate([gl, ql], 0))
        made = three(dot, (left_x[0, i], left_x[1, i]), right) * downs[span[i], :]
        dx_ref[span[i], :] = made + skip * g
        flow = jnp.sum(held[i] * carried, axis=0, keepdims=True)
        change = inner[span[i], :] - x * made + jnp.where(bottom, flow, 0.0)
        ch, cl = split(change)
        row_sums[span[i], :] += dot(ch, gather) + dot(cl, gather)
        acc_read[i] += three(dot_nt, (gh, gl), (right_h[i], right_l[i]))
        acc_write[i] += dot_nt(right_h[i, :CHUNK], jnp.concatenate([qh, ql], 0))
        acc_write[i, :, :state] += dot_nt(right_l[i, :CHUNK], qh)
        if i > 0:
            gained = dot(read_t[i], jnp.concatenate([gh, gh], 0)) + dot(read_t[i, :, :CHUNK], gl)
            carried = edge[i - 1][1:2] * (edge[i][0:1] * (carried + gained))

    @pl.when(step == last)
    def _():
        t, u = iota((CHUNK, CHUNK), 0), iota((CHUNK, CHUNK), 1)
        until = jnp.where(t >= u, 1.0, 0.0).astype(BF16)
        for i in range(count):
            scores = jnp.where(u <= t, acc_read[i, :, :CHUNK], 0.0)
            write, read = split(write_ref[span[i], :]), split(read_ref[span[i], :])
            grad_read = acc_read[i, :, CHUNK:] + three(dot, split(scores), write)
            grad_write = acc_write[i, :, :state] + acc_write[i, :, state:]
            grad_write = grad_write + three(dot, split(scores.T), read)
            parts = split3(row_sums[span[i], :].T)
            decay = sum(dot(p, until) for p in parts)[:heads]
            if chained:
                grad_read = grad_read + old_read[span[i], :]
                grad_write = grad_write + old_write[span[i], :]
                decay = decay + old_decay[:, span[i]]
            gr_ref[span[i], :] = grad_read
            gw_ref[span[i], :] = grad_write
            gd_ref[:, span[i]] = decay


def whole(shape):
    return pl.BlockSpec(shape, lambda *_: (0,) * len(shape))


def make_states(slot, log_decay, state_write, state_read, inputs, grad_output, first, blocks):
    rows, columns = inputs.shape
    heads, state = log_decay.shape[0], state_write.shape[1]
    quarter = state // 4
    pack = 128
    wide = pl.BlockSpec((rows, LANES), lambda j, _: (0, first + j))
    part = pl.BlockSpec((2, 2, quarter, LANES), lambda j, _: (0, 0, 0, j))
    shape = jax.ShapeDtypeStruct((2, 2, quarter, blocks * LANES), F32)
    width = columns // heads
    return pl.pallas_call(
        functools.partial(state_kernel, first_head=first * LANES // width, heads=heads, width=width),
        out_shape=(shape, shape),
        grid_spec=pltpu.PrefetchScalarGridSpec(
            num_scalar_prefetch=1,
            grid=(blocks,),
            in_specs=[
                whole((heads, rows)), whole((rows, state)), whole((rows, state)), wide, wide
            ],
            out_specs=(part, part),
            scratch_shapes=[
                pltpu.VMEM((pack, rows), F32),
                pltpu.VMEM((rows, pack), BF16),
                pltpu.VMEM((rows, pack), BF16),
                pltpu.VMEM((2, state, rows), BF16),
                pltpu.VMEM((2, state, rows), BF16),
                pltpu.VMEM((2, state, LANES), F32),
            ],
        ),
        compiler_params=pltpu.CompilerParams(vmem_limit_bytes=40 << 20),
        cost_estimate=pl.CostEstimate(
            flops=12 * rows * state * blocks * LANES,
            bytes_accessed=8 * rows * blocks * LANES,
            transcendentals=0,
        ),
    )(slot, log_decay, state_write, state_read, inputs, grad_output)


def make_outputs(
    slot, log_decay, state_write, state_read, skip, inputs, grad_output, mine, other, first, blocks,
    earlier
):
    rows, columns = inputs.shape
    heads, state = log_decay.shape[0], state_write.shape[1]
    quarter, count = state // 4, rows // CHUNK
    pack = 128
    wide = pl.BlockSpec((rows, LANES), lambda j, _: (0, first + j))
    part = pl.BlockSpec((2, 2, quarter, LANES), lambda j, _: (0, 0, 0, j))
    line = pl.BlockSpec((1, LANES), lambda j, _: (0, first + j))
    small = [whole((heads, rows)), whole((rows, state)), whole((rows, state))]
    in_specs = [*small, line, wide, wide, part, part]
    operands = [log_decay, state_write, state_read, skip, inputs, grad_output, mine, other]
    aliases = {}
    if earlier is not None:
        aliases = {9: 0, 10: 1}
        in_specs += [pl.BlockSpec(memory_space=pl.ANY)] * 2 + small
        operands += earlier
    width = columns // heads
    large = jax.ShapeDtypeStruct((rows, columns), F32)
    side = jax.ShapeDtypeStruct((rows, state), F32)
    return pl.pallas_call(
        functools.partial(
            block_kernel,
            first_head=first * LANES // width,
            heads=heads,
            width=width,
            chained=earlier is not None,
        ),
        out_shape=(large, large, jax.ShapeDtypeStruct((heads, rows), F32), side, side),
        grid_spec=pltpu.PrefetchScalarGridSpec(
            num_scalar_prefetch=1,
            grid=(blocks,),
            in_specs=in_specs,
            out_specs=(wide, wide, *small),
            scratch_shapes=[
                pltpu.VMEM((pack, rows), F32),
                pltpu.VMEM((rows, pack), BF16),
                pltpu.VMEM((rows, pack), BF16),
                pltpu.VMEM((count, 16, pack), BF16),
                pltpu.VMEM((2, count, CHUNK, CHUNK + state), BF16),
                pltpu.VMEM((2, count, CHUNK, CHUNK + state), BF16),
                pltpu.VMEM((count, state, 2 * CHUNK), BF16),
                pltpu.VMEM((count, state, 2 * CHUNK), BF16),
                pltpu.VMEM((rows, pack), F32),
                pltpu.VMEM((count, CHUNK, CHUNK + state), F32),
                pltpu.VMEM((count, CHUNK, 2 * state), F32),
                pltpu.VMEM((state, LANES), F32),
                pltpu.VMEM((state, LANES), F32),
                pltpu.VMEM((rows, LANES), F32),
                pltpu.VMEM((rows, LANES), F32),
                pltpu.VMEM((count, CHUNK + state, LANES), BF16),
                pltpu.VMEM((count, CHUNK + state, LANES), BF16),
                pltpu.VMEM((count, state, LANES), F32),
                pltpu.VMEM((rows, LANES), F32),
            ],
        ),
        input_output_aliases=aliases,
        compiler_params=pltpu.CompilerParams(vmem_limit_bytes=48 << 20),
        cost_estimate=pl.CostEstimate(
            flops=48 * rows * state * blocks * LANES,
            bytes_accessed=16 * rows * blocks * LANES,
            transcendentals=0,
        ),
    )(slot, *operands)


def local(inputs, log_decay, state_write, state_read, skip_gain, grad_output):
    heads = log_decay.shape[0]
    rows, columns = inputs.shape
    width = columns // heads
    devices, position = lax.axis_size("seq"), lax.axis_index("seq")
    planes = devices // 4
    core, chip, plane = position % 2, (position // 2) % 2, position // 4
    slot = (core * 2 + chip).astype(jnp.int32).reshape(1)
    swap_core = [(i, i ^ 1) for i in range(devices)]
    swap_chip = [(i, i ^ 2) for i in range(devices)]

    total = jnp.sum(log_decay, axis=1)
    twin = lax.ppermute(total, "seq", swap_core)
    here = total + twin
    beside = lax.ppermute(here, "seq", swap_chip)
    is_c0, is_y0 = core == 0, chip == 0
    logs = jnp.stack(
        [
            jnp.where(is_c0, total, twin),
            jnp.where(is_c0, twin, total),
            jnp.where(is_y0, here, beside),
            jnp.where(is_y0, beside, here),
            here + beside,
        ]
    )
    keepers = jnp.repeat(jnp.exp(logs), width, axis=1)
    one = jnp.ones((columns,), F32)
    skip = jnp.repeat(skip_gain, width).reshape(1, columns)

    def travel(first, blocks):
        lanes = slice(first * LANES, (first + blocks) * LANES)
        c0, c1, y0, y1, whole_plane = keepers[:, lanes]
        ones = one[lanes]
        keep, send = make_states(
            slot, log_decay, state_write, state_read, inputs, grad_output, first, blocks
        )
        near_core = lax.ppermute(send, "seq", swap_core)
        chip_f = jnp.where(is_c0, c1, ones) * keep[0] + jnp.where(is_c0, ones, c1) * near_core[0]
        chip_b = jnp.where(is_c0, ones, c0) * keep[1] + jnp.where(is_c0, c0, ones) * near_core[1]
        near_chip = lax.ppermute(jnp.stack([chip_f[1], chip_b[1]]), "seq", swap_chip)
        plane_f = jnp.where(is_y0, y1, ones) * chip_f[0] + jnp.where(is_y0, ones, y1) * near_chip[0]
        plane_b = jnp.where(is_y0, ones, y0) * chip_b[0] + jnp.where(is_y0, y0, ones) * near_chip[1]
        ahead = jnp.zeros_like(plane_f)
        back = jnp.zeros_like(plane_b)
        for hop in range(planes - 1):
            mirror = planes - 1 - hop
            going = jnp.where(
                plane == hop, whole_plane * ahead + plane_f, whole_plane * back + plane_b
            )
            pairs = [
                (source * 4 + i, target * 4 + i)
                for source, target in ((hop, hop + 1), (mirror, mirror - 1))
                for i in range(4)
            ]
            came = lax.ppermute(going, "seq", pairs)
            ahead = jnp.where(plane == hop + 1, came, ahead)
            back = jnp.where(plane == mirror - 1, came, back)
        mine = jnp.stack(
            [
                jnp.where(is_y0, ahead, y0 * ahead + near_chip[0]),
                jnp.where(is_y0, y1 * back + near_chip[1], back),
            ]
        )
        theirs = jnp.stack(
            [
                jnp.where(is_y0, y0 * ahead + chip_f[0], ahead),
                jnp.where(is_y0, back, y1 * back + chip_b[0]),
            ]
        )
        came = lax.ppermute(theirs, "seq", swap_chip)
        into_f = jnp.stack([mine[0], came[0]])
        into_b = jnp.stack([mine[1], came[1]])
        mine = jnp.stack(
            [
                jnp.where(is_c0, into_f, c0 * into_f + near_core[0]),
                jnp.where(is_c0, c1 * into_b + near_core[1], into_b),
            ]
        )
        theirs = jnp.stack(
            [
                jnp.where(is_c0, c0 * into_f + keep[0], into_f),
                jnp.where(is_c0, into_b, c1 * into_b + keep[1]),
            ]
        )
        return mine, lax.ppermute(theirs, "seq", swap_core)

    states = []
    first = 0
    for blocks in GROUPS:
        states.append((first, blocks, travel(first, blocks)))
        first += blocks
    results = None
    for first, blocks, (mine, other) in states:
        results = make_outputs(
            slot, log_decay, state_write, state_read, skip, inputs, grad_output, mine, other, first,
            blocks, results
        )
    outputs, grad_inputs, grad_decay, grad_write, grad_read = results
    return (outputs, grad_inputs, grad_decay, grad_write, grad_read)


def solution(mesh):
    in_specs = (
        P(("group", "seq"), None),
        P(None, ("group", "seq")),
        P(("group", "seq"), None),
        P(("group", "seq"), None),
        P(),
        P(("group", "seq"), None),
    )
    out_specs = (
        P(("group", "seq"), None),
        P(("group", "seq"), None),
        P(None, ("group", "seq")),
        P(("group", "seq"), None),
        P(("group", "seq"), None),
    )
    return jax.shard_map(local, mesh=mesh, in_specs=in_specs, out_specs=out_specs, check_vma=False)
```

```python
import functools
import math

import jax
import jax.numpy as jnp
from jax import lax
from jax.experimental import pallas as pl
from jax.experimental.pallas import tpu as pltpu
from jax.sharding import PartitionSpec as P

CHUNK = 128
LANES = 512
PACK = 128
GROUPS = (3, 2)
VMEM = 24 << 20
ANYWHERE = pl.BlockSpec(memory_space=pl.ANY)
F32 = jnp.float32
BF16 = jnp.bfloat16


def dot(a, b):
    return lax.dot_general(a, b, (((1,), (0,)), ((), ())), preferred_element_type=F32)


def dot_nt(a, b):
    return lax.dot_general(a, b, (((1,), (1,)), ((), ())), preferred_element_type=F32)


def split(x):
    high = x.astype(BF16)
    return high, (x - high.astype(F32)).astype(BF16)


def split3(x):
    high = x.astype(BF16)
    rest = x - high.astype(F32)
    middle = rest.astype(BF16)
    return high, middle, (rest - middle.astype(F32)).astype(BF16)


def three(product, a, b):
    return product(a[0], b[0]) + product(a[0], b[1]) + product(a[1], b[0])


def left3(x):
    high, low = split(x)
    return jnp.concatenate([high, high, low], 1)


def dot3(left, high, low):
    return dot(left, jnp.concatenate([high, low, high], 0))


def dot3_nt(a, high, low):
    return dot_nt(jnp.concatenate([a[0], a[0], a[1]], 1), jnp.concatenate([high, low, high], 1))


def iota(shape, axis):
    return lax.broadcasted_iota(jnp.int32, shape, axis)


def fold3(x, heads):
    high, middle, low = split3(x)
    column = iota(x.shape, 1)
    chosen = jnp.where(
        column < heads,
        high.astype(F32),
        jnp.where(column < 2 * heads, middle.astype(F32), low.astype(F32)),
    )
    return chosen.astype(BF16)


def spread_matrix(rows, lanes, first, heads, width):
    row, lane = iota((rows, lanes), 0), iota((rows, lanes), 1)
    hit = None
    for copy in range(3):
        start = (row - (first + copy * heads)) * width
        one = jnp.logical_and(lane >= start, lane < start + width)
        hit = one if hit is None else jnp.logical_or(hit, one)
    return jnp.where(hit, 1.0, 0.0).astype(BF16)


def pack_decay(packed, decay_ref, heads):
    packed[...] = jnp.zeros_like(packed)
    for copy in range(3):
        packed[copy * heads : (copy + 1) * heads, :] = decay_ref[...]


def state_kernel(
    slot_ref, decay_ref, write_ref, read_ref, x_ref, g_ref, *refs, groups, heads, width
):
    *out_refs, packed, tail, lead, write_t, read_t, stage = refs
    step = pl.program_id(0)
    rows, lanes = x_ref.shape
    state = write_ref.shape[1]
    quarter = state // 4

    @pl.when(step == 0)
    def _():
        pack_decay(packed, decay_ref, heads)
        parts = split3(packed[...])
        t, u = iota((rows, rows), 0), iota((rows, rows), 1)
        before = jnp.where(u <= t, 1.0, 0.0).astype(BF16)
        after = jnp.where(u > t, 1.0, 0.0).astype(BF16)
        lead[...] = fold3(jnp.exp(sum(dot_nt(before, p) for p in parts)), heads)
        tail[...] = fold3(jnp.exp(sum(dot_nt(after, p) for p in parts)), heads)
        write_t[...] = left3(write_ref[...].T)
        read_t[...] = left3(read_ref[...].T)

    first = step * (lanes // width)
    spread = spread_matrix(packed.shape[0], lanes, first, heads, width)
    slot = slot_ref[0]
    for which, (value_ref, weight, factor) in enumerate(
        ((x_ref, tail, write_t), (g_ref, lead, read_t))
    ):
        scaled = split(value_ref[...] * dot(weight[...], spread))
        stage[which] = dot3(factor[...], *scaled)
    begin = 0
    for k, blocks in enumerate(groups):

        @pl.when(jnp.logical_and(step >= begin, step < begin + blocks))
        def _(k=k):
            for which in range(2):
                for relative in range(4):
                    start = pl.multiple_of((slot ^ relative) * quarter, quarter)
                    target = out_refs[2 * k + relative // 2]
                    target[which, relative % 2] = stage[which, pl.ds(start, quarter), :]

        begin += blocks


def prepare_kernel(
    _early, _late, decay_ref, write_ref, read_ref, left_y, left_x, left_c, left_b, up, down, edges,
    packed
):
    heads, rows = decay_ref.shape
    middle = CHUNK // 2 - 1
    pack_decay(packed, decay_ref, heads)
    t, u = iota((CHUNK, CHUNK), 0), iota((CHUNK, CHUNK), 1)
    ahead = jnp.logical_and(u > middle, u <= t)
    behind = jnp.logical_and(u <= middle, u > t)
    signed = jnp.where(ahead, 1.0, jnp.where(behind, -1.0, 0.0)).astype(BF16)
    row, column = iota((16, CHUNK), 0), iota((16, CHUNK), 1)
    half = jnp.where((row == 0) == (column <= middle), 1.0, 0.0).astype(BF16)
    for i in range(rows // CHUNK):
        span = slice(i * CHUNK, (i + 1) * CHUNK)
        parts = split3(packed[:, span])
        gap = sum(dot_nt(signed, p) for p in parts)
        up[span, :] = fold3(jnp.exp(gap), heads)
        down[span, :] = fold3(jnp.exp(-gap), heads)
        edges[i] = fold3(jnp.exp(sum(dot_nt(half, p) for p in parts)), heads)
        write, read = write_ref[span, :], read_ref[span, :]
        write_p, read_p = split(write), split(read)
        scores = jnp.where(u <= t, three(dot_nt, read_p, write_p), 0.0)
        left_y[i] = left3(jnp.concatenate([scores, write.T], 0))
        scores = jnp.where(u >= t, three(dot_nt, write_p, read_p), 0.0)
        left_x[i] = left3(jnp.concatenate([scores, read.T], 0))
        left_c[i] = left3(read)
        left_b[i] = left3(write)


def block_kernel(
    slot_ref, left_y, left_x, left_c, left_b, up, down, edges, write_ref, read_ref, skip_ref,
    x_ref, g_ref, mine_ref, other_ref, *refs, first_head, heads, width, chained, closing
):
    if chained:
        _, _, old_read, old_write, old_sums, *refs = refs
    y_ref, dx_ref, acc_read, acc_write, sums, *refs = refs
    if closing:
        gd_ref, gw_ref, gr_ref, *refs = refs
    state_in, grad_in, ups, downs, right_h, right_l, held, inner = refs
    step, last = pl.program_id(0), pl.num_programs(0) - 1
    rows, lanes = x_ref.shape
    state = state_in.shape[0]
    quarter = state // 4
    count = rows // CHUNK
    span = [slice(i * CHUNK, (i + 1) * CHUNK) for i in range(count)]

    @pl.when(step == 0)
    def _():
        acc_read[...] = old_read[...] if chained else jnp.zeros_like(acc_read)
        acc_write[...] = old_write[...] if chained else jnp.zeros_like(acc_write)
        sums[...] = old_sums[...] if chained else jnp.zeros_like(sums)

    first = first_head + step * (lanes // width)
    spread = spread_matrix(PACK, lanes, first, heads, width)
    edge = [dot(edges[i], spread) for i in range(count)]
    skip = skip_ref[...]
    ups[...] = dot(up[...], spread)
    downs[...] = dot(down[...], spread)
    slot = slot_ref[0]
    for relative in range(4):
        start = pl.multiple_of((slot ^ relative) * quarter, quarter)
        source = mine_ref if relative < 2 else other_ref
        state_in[pl.ds(start, quarter), :] = source[0, relative % 2]
        grad_in[pl.ds(start, quarter), :] = source[1, relative % 2]

    carried = edge[0][0:1] * state_in[...]
    for i in range(count):
        x = x_ref[span[i], :]
        xh, xl = split(x * downs[span[i], :])
        ph, pl_ = split(carried)
        right_h[i, :CHUNK], right_l[i, :CHUNK] = xh, xl
        right_h[i, CHUNK:], right_l[i, CHUNK:] = ph, pl_
        both = dot3(left_y[i], xh, xl)
        made = (both[:CHUNK] + dot3(left_c[i], ph, pl_)) * ups[span[i], :]
        y_ref[span[i], :] = made + skip * x
        inner[span[i], :] = made * g_ref[span[i], :]
        total = carried + both[CHUNK:]
        held[i] = total
        if i + 1 < count:
            carried = edge[i + 1][0:1] * (edge[i][1:2] * total)

    row, lane = iota((lanes, PACK), 0), iota((lanes, PACK), 1)
    begin = (lane - first) * width
    gather = jnp.where(jnp.logical_and(row >= begin, row < begin + width), 1.0, 0.0).astype(BF16)
    bottom = iota((CHUNK, 1), 0) == CHUNK - 1
    carried = edge[count - 1][1:2] * grad_in[...]
    for i in reversed(range(count)):
        g, x = g_ref[span[i], :], x_ref[span[i], :]
        gh, gl = split(g * ups[span[i], :])
        qh, ql = split(carried)
        both = dot3(left_x[i] if i > 0 else left_x[i, :CHUNK], gh, gl)
        made = (both[:CHUNK] + dot3(left_b[i], qh, ql)) * downs[span[i], :]
        dx_ref[span[i], :] = made + skip * g
        flow = jnp.sum(held[i] * carried, axis=0, keepdims=True)
        ch, cl = split(inner[span[i], :] - x * made + jnp.where(bottom, flow, 0.0))
        sums[span[i], :] += dot(ch, gather) + dot(cl, gather)
        acc_read[i] += dot3_nt((right_h[i], right_l[i]), gh, gl)
        acc_write[i] += dot3_nt((right_h[i, :CHUNK], right_l[i, :CHUNK]), qh, ql)
        if i > 0:
            carried = edge[i - 1][1:2] * (edge[i][0:1] * (carried + both[CHUNK:]))

    if closing:

        @pl.when(step == last)
        def _():
            s, t = iota((CHUNK, CHUNK), 0), iota((CHUNK, CHUNK), 1)
            until = jnp.where(s >= t, 1.0, 0.0).astype(BF16)
            for i in range(count):
                scores = jnp.where(s <= t, acc_read[i, :CHUNK], 0.0)
                write, read = split(write_ref[span[i], :]), split(read_ref[span[i], :])
                gr_ref[span[i], :] = acc_read[i, CHUNK:].T + three(dot, split(scores.T), write)
                gw_ref[span[i], :] = acc_write[i] + three(dot, split(scores), read)
                parts = split3(sums[span[i], :].T)
                gd_ref[:, span[i]] = sum(dot(p, until) for p in parts)[:heads]


def whole(shape):
    return pl.BlockSpec(shape, lambda *_: (0,) * len(shape))


def make_states(slot, log_decay, state_write, state_read, inputs, grad_output, groups):
    rows, columns = inputs.shape
    heads, state = log_decay.shape[0], state_write.shape[1]
    quarter = state // 4
    wide = pl.BlockSpec((rows, LANES), lambda j, _: (0, j))
    shapes, specs, begin = [], [], 0
    for count in groups:
        shape = jax.ShapeDtypeStruct((2, 2, quarter, count * LANES), F32)
        spec = pl.BlockSpec(
            (2, 2, quarter, LANES),
            lambda j, _, begin=begin, count=count: (0, 0, 0, jnp.clip(j - begin, 0, count - 1)),
        )
        shapes += [shape, shape]
        specs += [spec, spec]
        begin += count
    blocks = begin
    width = columns // heads
    return pl.pallas_call(
        functools.partial(state_kernel, groups=groups, heads=heads, width=width),
        out_shape=tuple(shapes),
        grid_spec=pltpu.PrefetchScalarGridSpec(
            num_scalar_prefetch=1,
            grid=(blocks,),
            in_specs=[
                whole((heads, rows)), whole((rows, state)), whole((rows, state)), wide, wide
            ],
            out_specs=tuple(specs),
            scratch_shapes=[
                pltpu.VMEM((PACK, rows), F32),
                pltpu.VMEM((rows, PACK), BF16),
                pltpu.VMEM((rows, PACK), BF16),
                pltpu.VMEM((state, 3 * rows), BF16),
                pltpu.VMEM((state, 3 * rows), BF16),
                pltpu.VMEM((2, state, LANES), F32),
            ],
        ),
        compiler_params=pltpu.CompilerParams(vmem_limit_bytes=VMEM),
        cost_estimate=pl.CostEstimate(
            flops=12 * rows * state * blocks * LANES,
            bytes_accessed=8 * rows * blocks * LANES,
            transcendentals=0,
        ),
    )(slot, log_decay, state_write, state_read, inputs, grad_output)


def prepare(log_decay, state_write, state_read, early, late):
    heads, rows = log_decay.shape
    state = state_write.shape[1]
    count = rows // CHUNK
    left = jax.ShapeDtypeStruct((count, CHUNK + state, 3 * CHUNK), BF16)
    side = jax.ShapeDtypeStruct((count, CHUNK, 3 * state), BF16)
    column = jax.ShapeDtypeStruct((rows, PACK), BF16)
    edges = jax.ShapeDtypeStruct((count, 16, PACK), BF16)
    small = [whole((heads, rows)), whole((rows, state)), whole((rows, state))]
    return pl.pallas_call(
        prepare_kernel,
        in_specs=[ANYWHERE, ANYWHERE, *small],
        out_shape=(left, left, side, side, column, column, edges),
        scratch_shapes=[pltpu.VMEM((PACK, rows), F32)],
        cost_estimate=pl.CostEstimate(flops=1 << 30, bytes_accessed=6 << 20, transcendentals=0),
    )(early, late, log_decay, state_write, state_read)


def make_outputs(
    slot, prepared, skip, inputs, grad_output, pieces, heads, first, blocks, earlier, closing
):
    rows, columns = inputs.shape
    state = prepared[7].shape[1]
    quarter, count = state // 4, rows // CHUNK
    width = columns // heads
    wide = pl.BlockSpec((rows, LANES), lambda j, _: (0, first + j))
    part = pl.BlockSpec((2, 2, quarter, LANES), lambda j, _: (0, 0, 0, j))
    line = pl.BlockSpec((1, LANES), lambda j, _: (0, first + j))
    totals = [(count, CHUNK + state, CHUNK), (count, CHUNK, state), (rows, PACK)]
    in_specs = [*(whole(a.shape) for a in prepared), line, wide, wide, part, part]
    operands = [*prepared, skip, inputs, grad_output, *pieces]
    aliases = {}
    if earlier is not None:
        aliases = {len(operands) + 1: 0, len(operands) + 2: 1}
        in_specs += [ANYWHERE] * 2 + [whole(s) for s in totals]
        operands += earlier
    shapes = [(rows, columns)] * 2 + totals
    out_specs = [wide, wide, *(whole(s) for s in totals)]
    if closing:
        sides = [(heads, rows), (rows, state), (rows, state)]
        shapes += sides
        out_specs += [whole(s) for s in sides]
    return pl.pallas_call(
        functools.partial(
            block_kernel,
            first_head=first * LANES // width,
            heads=heads,
            width=width,
            chained=earlier is not None,
            closing=closing,
        ),
        out_shape=tuple(jax.ShapeDtypeStruct(s, F32) for s in shapes),
        grid_spec=pltpu.PrefetchScalarGridSpec(
            num_scalar_prefetch=1,
            grid=(blocks,),
            in_specs=in_specs,
            out_specs=tuple(out_specs),
            scratch_shapes=[
                pltpu.VMEM((state, LANES), F32),
                pltpu.VMEM((state, LANES), F32),
                pltpu.VMEM((rows, LANES), F32),
                pltpu.VMEM((rows, LANES), F32),
                pltpu.VMEM((count, CHUNK + state, LANES), BF16),
                pltpu.VMEM((count, CHUNK + state, LANES), BF16),
                pltpu.VMEM((count, state, LANES), F32),
                pltpu.VMEM((rows, LANES), F32),
            ],
        ),
        input_output_aliases=aliases,
        compiler_params=pltpu.CompilerParams(vmem_limit_bytes=28 << 20),
        cost_estimate=pl.CostEstimate(
            flops=140 * rows * state * blocks * LANES,
            bytes_accessed=16 * rows * blocks * LANES,
            transcendentals=0,
        ),
    )(slot, *operands)


def local(inputs, log_decay, state_write, state_read, skip_gain, grad_output):
    hbm = functools.partial(pltpu.with_memory_space_constraint, memory_space=pltpu.HBM)
    inputs, grad_output = hbm(inputs), hbm(grad_output)
    state_write, state_read = hbm(state_write), hbm(state_read)
    heads = log_decay.shape[0]
    rows, columns = inputs.shape
    width = columns // heads
    devices, position = lax.axis_size("seq"), lax.axis_index("seq")
    planes = devices // 4
    core, chip, plane = position % 2, (position // 2) % 2, position // 4
    slot = (core * 2 + chip).astype(jnp.int32).reshape(1)
    swap_core = [(i, i ^ 1) for i in range(devices)]
    swap_chip = [(i, i ^ 2) for i in range(devices)]

    total = jnp.sum(log_decay, axis=1)
    twin, beside, across = (
        lax.ppermute(total, "seq", [(i, i ^ bits) for i in range(devices)]) for bits in (1, 2, 3)
    )
    here, there = total + twin, beside + across
    is_c0, is_y0 = core == 0, chip == 0
    logs = jnp.stack(
        [
            jnp.where(is_c0, total, twin),
            jnp.where(is_c0, twin, total),
            jnp.where(is_y0, here, there),
            jnp.where(is_y0, there, here),
            here + there,
        ]
    )
    keepers = jnp.repeat(jnp.exp(logs), width, axis=1)
    one = jnp.ones((columns,), F32)
    skip = jnp.repeat(skip_gain, width).reshape(1, columns)

    goings = []
    made = make_states(slot, log_decay, state_write, state_read, inputs, grad_output, GROUPS)

    def travel(first, blocks, keep, send):
        lanes = slice(first * LANES, (first + blocks) * LANES)
        c0, c1, y0, y1, whole_plane = keepers[:, lanes]
        ones = one[lanes]
        near_core = lax.ppermute(send, "seq", swap_core)
        chip_f = jnp.where(is_c0, c1, ones) * keep[0] + jnp.where(is_c0, ones, c1) * near_core[0]
        chip_b = jnp.where(is_c0, ones, c0) * keep[1] + jnp.where(is_c0, c0, ones) * near_core[1]
        going = jnp.stack([chip_f[1], chip_b[1]])
        near_chip = lax.ppermute(going, "seq", swap_chip)
        if not goings:
            goings.append(prepare(log_decay, state_write, state_read, skip, going))
            near_chip, _ = lax.optimization_barrier((near_chip, goings[0][-1]))
        plane_f = jnp.where(is_y0, y1, ones) * chip_f[0] + jnp.where(is_y0, ones, y1) * near_chip[0]
        plane_b = jnp.where(is_y0, ones, y0) * chip_b[0] + jnp.where(is_y0, y0, ones) * near_chip[1]
        ahead = jnp.zeros_like(plane_f)
        back = jnp.zeros_like(plane_b)
        for hop in range(planes - 1):
            mirror = planes - 1 - hop
            going = jnp.where(
                plane == hop, whole_plane * ahead + plane_f, whole_plane * back + plane_b
            )
            pairs = [
                (source * 4 + i, target * 4 + i)
                for source, target in ((hop, hop + 1), (mirror, mirror - 1))
                for i in range(4)
            ]
            came = lax.ppermute(going, "seq", pairs)
            ahead = jnp.where(plane == hop + 1, came, ahead)
            back = jnp.where(plane == mirror - 1, came, back)
        mine = jnp.stack(
            [
                jnp.where(is_y0, ahead, y0 * ahead + near_chip[0]),
                jnp.where(is_y0, y1 * back + near_chip[1], back),
            ]
        )
        theirs = jnp.stack(
            [
                jnp.where(is_y0, y0 * ahead + chip_f[0], ahead),
                jnp.where(is_y0, back, y1 * back + chip_b[0]),
            ]
        )
        came = lax.ppermute(theirs, "seq", swap_chip)
        into_f = jnp.stack([mine[0], came[0]])
        into_b = jnp.stack([mine[1], came[1]])
        mine = jnp.stack(
            [
                jnp.where(is_c0, into_f, c0 * into_f + near_core[0]),
                jnp.where(is_c0, c1 * into_b + near_core[1], into_b),
            ]
        )
        theirs = jnp.stack(
            [
                jnp.where(is_c0, c0 * into_f + keep[0], into_f),
                jnp.where(is_c0, into_b, c1 * into_b + keep[1]),
            ]
        )
        return mine, lax.ppermute(theirs, "seq", swap_core)

    travels = []
    first = 0
    for k, blocks in enumerate(GROUPS):
        pair = made[2 * k : 2 * k + 2]
        travels.append((first, blocks, travel(first, blocks, *pair)))
        first += blocks
    prepared = [*goings[0], state_write, state_read]
    results = None
    for k, (first, blocks, pieces) in enumerate(travels):
        results = make_outputs(
            slot, prepared, skip, inputs, grad_output, pieces, heads, first, blocks, results,
            k + 1 == len(travels)
        )
    outputs, grad_inputs, _, _, _, grad_decay, grad_write, grad_read = results
    return (outputs, grad_inputs, grad_decay, grad_write, grad_read)


def solution(mesh):
    in_specs = (
        P(("group", "seq"), None),
        P(None, ("group", "seq")),
        P(("group", "seq"), None),
        P(("group", "seq"), None),
        P(),
        P(("group", "seq"), None),
    )
    out_specs = (
        P(("group", "seq"), None),
        P(("group", "seq"), None),
        P(None, ("group", "seq")),
        P(("group", "seq"), None),
        P(("group", "seq"), None),
    )
    return jax.shard_map(local, mesh=mesh, in_specs=in_specs, out_specs=out_specs, check_vma=False)
```

```python
import functools
import math

import jax
import jax.numpy as jnp
from jax import lax
from jax.experimental import pallas as pl
from jax.experimental.pallas import tpu as pltpu
from jax.sharding import PartitionSpec as P

CHUNK = 128
LANES = 512
PACK = 128
GROUPS = (3, 2)
VMEM = 24 << 20
ANYWHERE = pl.BlockSpec(memory_space=pl.ANY)
F32 = jnp.float32
BF16 = jnp.bfloat16


def dot(a, b):
    return lax.dot_general(a, b, (((1,), (0,)), ((), ())), preferred_element_type=F32)


def dot_nt(a, b):
    return lax.dot_general(a, b, (((1,), (1,)), ((), ())), preferred_element_type=F32)


def split(x):
    high = x.astype(BF16)
    return high, (x - high.astype(F32)).astype(BF16)


def split3(x):
    high = x.astype(BF16)
    rest = x - high.astype(F32)
    middle = rest.astype(BF16)
    return high, middle, (rest - middle.astype(F32)).astype(BF16)


def three(product, a, b):
    return product(a[0], b[0]) + product(a[0], b[1]) + product(a[1], b[0])


def left3(x):
    high, low = split(x)
    return jnp.concatenate([high, high, low], 1)


def dot3(left, high, low):
    depth = left.shape[1] // 3
    a, b = left[:, :depth], left[:, 2 * depth :]
    rows = left.shape[0]
    both = dot(
        jnp.concatenate([jnp.concatenate([a, a], 1), jnp.concatenate([b, b], 1)], 0),
        jnp.concatenate([high, low], 0),
    )
    return both[:rows] + both[rows:]


def dot3_nt(a, high, low):
    rows = a[0].shape[0]
    both = dot_nt(jnp.concatenate([a[0], a[1]], 0), high)
    return both[:rows] + both[rows:] + dot_nt(a[0], low)


def iota(shape, axis):
    return lax.broadcasted_iota(jnp.int32, shape, axis)


def fold3(x, heads):
    high, middle, low = split3(x)
    column = iota(x.shape, 1)
    chosen = jnp.where(
        column < heads,
        high.astype(F32),
        jnp.where(column < 2 * heads, middle.astype(F32), low.astype(F32)),
    )
    return chosen.astype(BF16)


def spread_matrix(rows, lanes, first, heads, width):
    row, lane = iota((rows, lanes), 0), iota((rows, lanes), 1)
    hit = None
    for copy in range(3):
        start = (row - (first + copy * heads)) * width
        one = jnp.logical_and(lane >= start, lane < start + width)
        hit = one if hit is None else jnp.logical_or(hit, one)
    return jnp.where(hit, 1.0, 0.0).astype(BF16)


def pack_decay(packed, decay_ref, heads):
    packed[...] = jnp.zeros_like(packed)
    for copy in range(3):
        packed[copy * heads : (copy + 1) * heads, :] = decay_ref[...]


def state_kernel(
    slot_ref, decay_ref, write_ref, read_ref, x_ref, g_ref, *refs, groups, heads, width
):
    *out_refs, packed, tail, lead, write_t, read_t, stage = refs
    step = pl.program_id(0)
    rows, lanes = x_ref.shape
    state = write_ref.shape[1]
    quarter = state // 4

    @pl.when(step == 0)
    def _():
        pack_decay(packed, decay_ref, heads)
        parts = split3(packed[...])
        t, u = iota((rows, rows), 0), iota((rows, rows), 1)
        before = jnp.where(u <= t, 1.0, 0.0).astype(BF16)
        after = jnp.where(u > t, 1.0, 0.0).astype(BF16)
        lead[...] = fold3(jnp.exp(sum(dot_nt(before, p) for p in parts)), heads)
        tail[...] = fold3(jnp.exp(sum(dot_nt(after, p) for p in parts)), heads)
        write_t[...] = left3(write_ref[...].T)
        read_t[...] = left3(read_ref[...].T)

    first = step * (lanes // width)
    spread = spread_matrix(packed.shape[0], lanes, first, heads, width)
    slot = slot_ref[0]
    for which, (value_ref, weight, factor) in enumerate(
        ((x_ref, tail, write_t), (g_ref, lead, read_t))
    ):
        scaled = split(value_ref[...] * dot(weight[...], spread))
        stage[which] = dot3(factor[...], *scaled)
    begin = 0
    for k, blocks in enumerate(groups):

        @pl.when(jnp.logical_and(step >= begin, step < begin + blocks))
        def _(k=k):
            for which in range(2):
                for relative in range(4):
                    start = pl.multiple_of((slot ^ relative) * quarter, quarter)
                    target = out_refs[2 * k + relative // 2]
                    target[which, relative % 2] = stage[which, pl.ds(start, quarter), :]

        begin += blocks


def prepare_kernel(
    _early, _late, decay_ref, write_ref, read_ref, left_y, left_x, left_c, left_b, up, down, edges,
    packed
):
    heads, rows = decay_ref.shape
    middle = CHUNK // 2 - 1
    pack_decay(packed, decay_ref, heads)
    t, u = iota((CHUNK, CHUNK), 0), iota((CHUNK, CHUNK), 1)
    ahead = jnp.logical_and(u > middle, u <= t)
    behind = jnp.logical_and(u <= middle, u > t)
    signed = jnp.where(ahead, 1.0, jnp.where(behind, -1.0, 0.0)).astype(BF16)
    row, column = iota((16, CHUNK), 0), iota((16, CHUNK), 1)
    half = jnp.where((row == 0) == (column <= middle), 1.0, 0.0).astype(BF16)
    for i in range(rows // CHUNK):
        span = slice(i * CHUNK, (i + 1) * CHUNK)
        parts = split3(packed[:, span])
        gap = sum(dot_nt(signed, p) for p in parts)
        up[span, :] = fold3(jnp.exp(gap), heads)
        down[span, :] = fold3(jnp.exp(-gap), heads)
        edges[i] = fold3(jnp.exp(sum(dot_nt(half, p) for p in parts)), heads)
        write, read = write_ref[span, :], read_ref[span, :]
        write_p, read_p = split(write), split(read)
        scores = jnp.where(u <= t, three(dot_nt, read_p, write_p), 0.0)
        left_y[i] = left3(jnp.concatenate([scores, write.T], 0))
        scores = jnp.where(u >= t, three(dot_nt, write_p, read_p), 0.0)
        left_x[i] = left3(jnp.concatenate([scores, read.T], 0))
        left_c[i] = left3(read)
        left_b[i] = left3(write)


def fold_pair(a, b, size):
    lower = iota(a.shape, 1) % (2 * size) < size
    return jnp.where(
        lower, a + pltpu.roll(a, PACK - size, 1), b + pltpu.roll(b, size, 1)
    )


def fold_heads(x):
    tiles = [x[:, k * PACK : (k + 1) * PACK] for k in range(4)]
    return fold_pair(fold_pair(tiles[0], tiles[1], 32), fold_pair(tiles[2], tiles[3], 32), 16)


def gather_matrix(first):
    lane, column = iota((2 * PACK, PACK), 0) % PACK, iota((2 * PACK, PACK), 1)
    head = lane % 32 // 16 * 4 + lane % 64 // 32 * 2 + lane // 64
    return jnp.where(column == first + head, 1.0, 0.0).astype(BF16)


def block_kernel(
    slot_ref, left_y, left_x, left_c, left_b, up, down, edges, write_ref, read_ref, skip_ref,
    x_ref, g_ref, mine_ref, other_ref, *refs, first_head, heads, width, chained, closing
):
    if chained:
        _, _, old_read, old_write, old_sums, *refs = refs
    y_ref, dx_ref, acc_read, acc_write, sums, *refs = refs
    if closing:
        gd_ref, gw_ref, gr_ref, *refs = refs
    (
        state_in, grad_in, ups, downs, right_h, right_l, held, inner, folded, turned_h, turned_l,
        ends, outer
    ) = refs
    step, last = pl.program_id(0), pl.num_programs(0) - 1
    rows, lanes = x_ref.shape
    state = state_in.shape[0]
    quarter = state // 4
    count = rows // CHUNK
    span = [slice(i * CHUNK, (i + 1) * CHUNK) for i in range(count)]

    @pl.when(step == 0)
    def _():
        acc_read[...] = old_read[...] if chained else jnp.zeros_like(acc_read)
        acc_write[...] = old_write[...] if chained else jnp.zeros_like(acc_write)
        sums[...] = old_sums[...] if chained else jnp.zeros_like(sums)

    first = first_head + step * (lanes // width)
    spread = spread_matrix(PACK, lanes, first, heads, width)
    edge = [dot(edges[i], spread) for i in range(count)]
    skip = skip_ref[...]
    ups[...] = dot(up[...], spread)
    downs[...] = dot(down[...], spread)
    slot = slot_ref[0]
    for relative in range(4):
        start = pl.multiple_of((slot ^ relative) * quarter, quarter)
        source = mine_ref if relative < 2 else other_ref
        state_in[pl.ds(start, quarter), :] = source[0, relative % 2]
        grad_in[pl.ds(start, quarter), :] = source[1, relative % 2]

    ahead = edge[0][0:1] * state_in[...]
    back = edge[count - 1][1:2] * grad_in[...]
    for i in range(count):
        x, g = x_ref[span[i], :], g_ref[span[i], :]
        xh, xl = split(x * downs[span[i], :])
        ph, pl_ = split(ahead)
        right_h[i, :CHUNK], right_l[i, :CHUNK] = xh, xl
        right_h[i, CHUNK:], right_l[i, CHUNK:] = ph, pl_
        both = dot3(left_y[i], xh, xl)
        made = (both[:CHUNK] + dot3(left_c[i], ph, pl_)) * ups[span[i], :]
        y_ref[span[i], :] = made + skip * x
        inner[span[i], :] = made * g
        total = ahead + both[CHUNK:]
        held[i] = total
        if i + 1 < count:
            ahead = edge[i + 1][0:1] * (edge[i][1:2] * total)

        j = count - 1 - i
        x, g = x_ref[span[j], :], g_ref[span[j], :]
        gh, gl = split(g * ups[span[j], :])
        qh, ql = split(back)
        turned_h[j, :CHUNK], turned_l[j, :CHUNK] = gh, gl
        turned_h[j, CHUNK:], turned_l[j, CHUNK:] = qh, ql
        both = dot3(left_x[j] if j > 0 else left_x[j, :CHUNK], gh, gl)
        made = (both[:CHUNK] + dot3(left_b[j], qh, ql)) * downs[span[j], :]
        dx_ref[span[j], :] = made + skip * g
        outer[span[j], :] = x * made
        ends[j] = back
        if j > 0:
            back = edge[j - 1][1:2] * (edge[j][0:1] * (back + both[CHUNK:]))

    bottom = iota((CHUNK, 1), 0) == CHUNK - 1
    for i in range(count):
        flow = jnp.sum(held[i] * ends[i], axis=0, keepdims=True)
        change = inner[span[i], :] - outer[span[i], :] + jnp.where(bottom, flow, 0.0)
        folded[span[i], :] = fold_heads(change)
        pairs = dot3_nt((right_h[i], right_l[i]), turned_h[i], turned_l[i])
        acc_read[i] += pairs[:, :CHUNK]
        acc_write[i] += pairs[:CHUNK, CHUNK:]

    ch, cl = split(folded[...])
    sums[...] += dot(jnp.concatenate([ch, cl], 1), gather_matrix(first))

    if closing:

        @pl.when(step == last)
        def _():
            s, t = iota((CHUNK, CHUNK), 0), iota((CHUNK, CHUNK), 1)
            until = jnp.where(s >= t, 1.0, 0.0).astype(BF16)
            for i in range(count):
                scores = jnp.where(s <= t, acc_read[i, :CHUNK], 0.0)
                write, read = split(write_ref[span[i], :]), split(read_ref[span[i], :])
                gr_ref[span[i], :] = acc_read[i, CHUNK:].T + three(dot, split(scores.T), write)
                gw_ref[span[i], :] = acc_write[i] + three(dot, split(scores), read)
                parts = split3(sums[span[i], :].T)
                gd_ref[:, span[i]] = sum(dot(p, until) for p in parts)[:heads]


def whole(shape):
    return pl.BlockSpec(shape, lambda *_: (0,) * len(shape))


def make_states(slot, log_decay, state_write, state_read, inputs, grad_output, groups):
    rows, columns = inputs.shape
    heads, state = log_decay.shape[0], state_write.shape[1]
    quarter = state // 4
    wide = pl.BlockSpec((rows, LANES), lambda j, _: (0, j))
    shapes, specs, begin = [], [], 0
    for count in groups:
        shape = jax.ShapeDtypeStruct((2, 2, quarter, count * LANES), F32)
        spec = pl.BlockSpec(
            (2, 2, quarter, LANES),
            lambda j, _, begin=begin, count=count: (0, 0, 0, jnp.clip(j - begin, 0, count - 1)),
        )
        shapes += [shape, shape]
        specs += [spec, spec]
        begin += count
    blocks = begin
    width = columns // heads
    return pl.pallas_call(
        functools.partial(state_kernel, groups=groups, heads=heads, width=width),
        out_shape=tuple(shapes),
        grid_spec=pltpu.PrefetchScalarGridSpec(
            num_scalar_prefetch=1,
            grid=(blocks,),
            in_specs=[
                whole((heads, rows)), whole((rows, state)), whole((rows, state)), wide, wide
            ],
            out_specs=tuple(specs),
            scratch_shapes=[
                pltpu.VMEM((PACK, rows), F32),
                pltpu.VMEM((rows, PACK), BF16),
                pltpu.VMEM((rows, PACK), BF16),
                pltpu.VMEM((state, 3 * rows), BF16),
                pltpu.VMEM((state, 3 * rows), BF16),
                pltpu.VMEM((2, state, LANES), F32),
            ],
        ),
        compiler_params=pltpu.CompilerParams(vmem_limit_bytes=VMEM),
        cost_estimate=pl.CostEstimate(
            flops=12 * rows * state * blocks * LANES,
            bytes_accessed=8 * rows * blocks * LANES,
            transcendentals=0,
        ),
    )(slot, log_decay, state_write, state_read, inputs, grad_output)


def prepare(log_decay, state_write, state_read, early, late):
    heads, rows = log_decay.shape
    state = state_write.shape[1]
    count = rows // CHUNK
    left = jax.ShapeDtypeStruct((count, CHUNK + state, 3 * CHUNK), BF16)
    side = jax.ShapeDtypeStruct((count, CHUNK, 3 * state), BF16)
    column = jax.ShapeDtypeStruct((rows, PACK), BF16)
    edges = jax.ShapeDtypeStruct((count, 16, PACK), BF16)
    small = [whole((heads, rows)), whole((rows, state)), whole((rows, state))]
    return pl.pallas_call(
        prepare_kernel,
        in_specs=[ANYWHERE, ANYWHERE, *small],
        out_shape=(left, left, side, side, column, column, edges),
        scratch_shapes=[pltpu.VMEM((PACK, rows), F32)],
        cost_estimate=pl.CostEstimate(flops=1 << 30, bytes_accessed=6 << 20, transcendentals=0),
    )(early, late, log_decay, state_write, state_read)


def make_outputs(
    slot, prepared, skip, inputs, grad_output, pieces, heads, first, blocks, earlier, closing
):
    rows, columns = inputs.shape
    state = prepared[7].shape[1]
    quarter, count = state // 4, rows // CHUNK
    width = columns // heads
    wide = pl.BlockSpec((rows, LANES), lambda j, _: (0, first + j))
    part = pl.BlockSpec((2, 2, quarter, LANES), lambda j, _: (0, 0, 0, j))
    line = pl.BlockSpec((1, LANES), lambda j, _: (0, first + j))
    totals = [(count, CHUNK + state, CHUNK), (count, CHUNK, state), (rows, PACK)]
    in_specs = [*(whole(a.shape) for a in prepared), line, wide, wide, part, part]
    operands = [*prepared, skip, inputs, grad_output, *pieces]
    aliases = {}
    if earlier is not None:
        aliases = {len(operands) + 1: 0, len(operands) + 2: 1}
        in_specs += [ANYWHERE] * 2 + [whole(s) for s in totals]
        operands += earlier
    shapes = [(rows, columns)] * 2 + totals
    out_specs = [wide, wide, *(whole(s) for s in totals)]
    if closing:
        sides = [(heads, rows), (rows, state), (rows, state)]
        shapes += sides
        out_specs += [whole(s) for s in sides]
    return pl.pallas_call(
        functools.partial(
            block_kernel,
            first_head=first * LANES // width,
            heads=heads,
            width=width,
            chained=earlier is not None,
            closing=closing,
        ),
        out_shape=tuple(jax.ShapeDtypeStruct(s, F32) for s in shapes),
        grid_spec=pltpu.PrefetchScalarGridSpec(
            num_scalar_prefetch=1,
            grid=(blocks,),
            in_specs=in_specs,
            out_specs=tuple(out_specs),
            scratch_shapes=[
                pltpu.VMEM((state, LANES), F32),
                pltpu.VMEM((state, LANES), F32),
                pltpu.VMEM((rows, LANES), F32),
                pltpu.VMEM((rows, LANES), F32),
                pltpu.VMEM((count, CHUNK + state, LANES), BF16),
                pltpu.VMEM((count, CHUNK + state, LANES), BF16),
                pltpu.VMEM((count, state, LANES), F32),
                pltpu.VMEM((rows, LANES), F32),
                pltpu.VMEM((rows, PACK), F32),
                pltpu.VMEM((count, CHUNK + state, LANES), BF16),
                pltpu.VMEM((count, CHUNK + state, LANES), BF16),
                pltpu.VMEM((count, state, LANES), F32),
                pltpu.VMEM((rows, LANES), F32),
            ],
        ),
        input_output_aliases=aliases,
        compiler_params=pltpu.CompilerParams(vmem_limit_bytes=32 << 20),
        cost_estimate=pl.CostEstimate(
            flops=140 * rows * state * blocks * LANES,
            bytes_accessed=16 * rows * blocks * LANES,
            transcendentals=0,
        ),
    )(slot, *operands)


def local(inputs, log_decay, state_write, state_read, skip_gain, grad_output):
    hbm = functools.partial(pltpu.with_memory_space_constraint, memory_space=pltpu.HBM)
    inputs, grad_output = hbm(inputs), hbm(grad_output)
    state_write, state_read = hbm(state_write), hbm(state_read)
    heads = log_decay.shape[0]
    rows, columns = inputs.shape
    width = columns // heads
    devices, position = lax.axis_size("seq"), lax.axis_index("seq")
    planes = devices // 4
    core, chip, plane = position % 2, (position // 2) % 2, position // 4
    slot = (core * 2 + chip).astype(jnp.int32).reshape(1)
    swap_core = [(i, i ^ 1) for i in range(devices)]
    swap_chip = [(i, i ^ 2) for i in range(devices)]

    total = jnp.sum(log_decay, axis=1)
    twin, beside, across = (
        lax.ppermute(total, "seq", [(i, i ^ bits) for i in range(devices)]) for bits in (1, 2, 3)
    )
    here, there = total + twin, beside + across
    is_c0, is_y0 = core == 0, chip == 0
    logs = jnp.stack(
        [
            jnp.where(is_c0, total, twin),
            jnp.where(is_c0, twin, total),
            jnp.where(is_y0, here, there),
            jnp.where(is_y0, there, here),
            here + there,
        ]
    )
    keepers = jnp.repeat(jnp.exp(logs), width, axis=1)
    one = jnp.ones((columns,), F32)
    skip = jnp.repeat(skip_gain, width).reshape(1, columns)

    goings = []
    made = make_states(slot, log_decay, state_write, state_read, inputs, grad_output, GROUPS)

    def travel(first, blocks, keep, send):
        lanes = slice(first * LANES, (first + blocks) * LANES)
        c0, c1, y0, y1, whole_plane = keepers[:, lanes]
        ones = one[lanes]
        near_core = lax.ppermute(send, "seq", swap_core)
        chip_f = jnp.where(is_c0, c1, ones) * keep[0] + jnp.where(is_c0, ones, c1) * near_core[0]
        chip_b = jnp.where(is_c0, ones, c0) * keep[1] + jnp.where(is_c0, c0, ones) * near_core[1]
        going = jnp.stack([chip_f[1], chip_b[1]])
        near_chip = lax.ppermute(going, "seq", swap_chip)
        if not goings:
            goings.append(prepare(log_decay, state_write, state_read, skip, going))
            near_chip, _ = lax.optimization_barrier((near_chip, goings[0][-1]))
        plane_f = jnp.where(is_y0, y1, ones) * chip_f[0] + jnp.where(is_y0, ones, y1) * near_chip[0]
        plane_b = jnp.where(is_y0, ones, y0) * chip_b[0] + jnp.where(is_y0, y0, ones) * near_chip[1]
        ahead = jnp.zeros_like(plane_f)
        back = jnp.zeros_like(plane_b)
        for hop in range(planes - 1):
            mirror = planes - 1 - hop
            going = jnp.where(
                plane == hop, whole_plane * ahead + plane_f, whole_plane * back + plane_b
            )
            pairs = [
                (source * 4 + i, target * 4 + i)
                for source, target in ((hop, hop + 1), (mirror, mirror - 1))
                for i in range(4)
            ]
            came = lax.ppermute(going, "seq", pairs)
            ahead = jnp.where(plane == hop + 1, came, ahead)
            back = jnp.where(plane == mirror - 1, came, back)
        mine = jnp.stack(
            [
                jnp.where(is_y0, ahead, y0 * ahead + near_chip[0]),
                jnp.where(is_y0, y1 * back + near_chip[1], back),
            ]
        )
        theirs = jnp.stack(
            [
                jnp.where(is_y0, y0 * ahead + chip_f[0], ahead),
                jnp.where(is_y0, back, y1 * back + chip_b[0]),
            ]
        )
        came = lax.ppermute(theirs, "seq", swap_chip)
        into_f = jnp.stack([mine[0], came[0]])
        into_b = jnp.stack([mine[1], came[1]])
        mine = jnp.stack(
            [
                jnp.where(is_c0, into_f, c0 * into_f + near_core[0]),
                jnp.where(is_c0, c1 * into_b + near_core[1], into_b),
            ]
        )
        theirs = jnp.stack(
            [
                jnp.where(is_c0, c0 * into_f + keep[0], into_f),
                jnp.where(is_c0, into_b, c1 * into_b + keep[1]),
            ]
        )
        return mine, lax.ppermute(theirs, "seq", swap_core)

    travels = []
    first = 0
    for k, blocks in enumerate(GROUPS):
        pair = made[2 * k : 2 * k + 2]
        travels.append((first, blocks, travel(first, blocks, *pair)))
        first += blocks
    prepared = [*goings[0], state_write, state_read]
    results = None
    for k, (first, blocks, pieces) in enumerate(travels):
        results = make_outputs(
            slot, prepared, skip, inputs, grad_output, pieces, heads, first, blocks, results,
            k + 1 == len(travels)
        )
    outputs, grad_inputs, _, _, _, grad_decay, grad_write, grad_read = results
    return (outputs, grad_inputs, grad_decay, grad_write, grad_read)


def solution(mesh):
    in_specs = (
        P(("group", "seq"), None),
        P(None, ("group", "seq")),
        P(("group", "seq"), None),
        P(("group", "seq"), None),
        P(),
        P(("group", "seq"), None),
    )
    out_specs = (
        P(("group", "seq"), None),
        P(("group", "seq"), None),
        P(None, ("group", "seq")),
        P(("group", "seq"), None),
        P(("group", "seq"), None),
    )
    return jax.shard_map(local, mesh=mesh, in_specs=in_specs, out_specs=out_specs, check_vma=False)
```

```python
import functools
import math

import jax
import jax.numpy as jnp
from jax import lax
from jax.experimental import pallas as pl
from jax.experimental.pallas import tpu as pltpu
from jax.sharding import PartitionSpec as P

CHUNK = 128
LANES = 512
PACK = 128
GROUPS = (3, 2)
VMEM = 24 << 20
ANYWHERE = pl.BlockSpec(memory_space=pl.ANY)
F32 = jnp.float32
BF16 = jnp.bfloat16


def dot(a, b):
    return lax.dot_general(a, b, (((1,), (0,)), ((), ())), preferred_element_type=F32)


def dot_nt(a, b):
    return lax.dot_general(a, b, (((1,), (1,)), ((), ())), preferred_element_type=F32)


def split(x):
    high = x.astype(BF16)
    return high, (x - high.astype(F32)).astype(BF16)


def split3(x):
    high = x.astype(BF16)
    rest = x - high.astype(F32)
    middle = rest.astype(BF16)
    return high, middle, (rest - middle.astype(F32)).astype(BF16)


def three(product, a, b):
    return product(a[0], b[0]) + product(a[0], b[1]) + product(a[1], b[0])


def left3(x):
    high, low = split(x)
    return jnp.concatenate([high, high, low], 1)


def dot3(left, high, low):
    depth = left.shape[1] // 3
    a, b = left[:, :depth], left[:, 2 * depth :]
    rows = left.shape[0]
    both = dot(
        jnp.concatenate([jnp.concatenate([a, a], 1), jnp.concatenate([b, b], 1)], 0),
        jnp.concatenate([high, low], 0),
    )
    return both[:rows] + both[rows:]


def dot3_nt(a, high, low):
    rows = a[0].shape[0]
    both = dot_nt(jnp.concatenate([a[0], a[1]], 0), high)
    return both[:rows] + both[rows:] + dot_nt(a[0], low)


def iota(shape, axis):
    return lax.broadcasted_iota(jnp.int32, shape, axis)


def fold3(x, heads):
    high, middle, low = split3(x)
    column = iota(x.shape, 1)
    chosen = jnp.where(
        column < heads,
        high.astype(F32),
        jnp.where(column < 2 * heads, middle.astype(F32), low.astype(F32)),
    )
    return chosen.astype(BF16)


def spread_matrix(rows, lanes, first, heads, width):
    row, lane = iota((rows, lanes), 0), iota((rows, lanes), 1)
    hit = None
    for copy in range(3):
        start = (row - (first + copy * heads)) * width
        one = jnp.logical_and(lane >= start, lane < start + width)
        hit = one if hit is None else jnp.logical_or(hit, one)
    return jnp.where(hit, 1.0, 0.0).astype(BF16)


def pack_decay(packed, decay_ref, heads):
    packed[...] = jnp.zeros_like(packed)
    for copy in range(3):
        packed[copy * heads : (copy + 1) * heads, :] = decay_ref[...]


def state_kernel(
    slot_ref, decay_ref, write_ref, read_ref, x_ref, g_ref, *refs, groups, heads, width
):
    *out_refs, decay_out, packed, tail, lead, write_t, read_t, stage = refs
    step = pl.program_id(0)
    rows, lanes = x_ref.shape
    state = write_ref.shape[1]
    quarter = state // 4

    @pl.when(step == 0)
    def _():
        pack_decay(packed, decay_ref, heads)
        parts = split3(packed[...])
        t, u = iota((rows, rows), 0), iota((rows, rows), 1)
        before = jnp.where(u <= t, 1.0, 0.0).astype(BF16)
        after = jnp.where(u > t, 1.0, 0.0).astype(BF16)
        lead[...] = fold3(jnp.exp(sum(dot_nt(before, p) for p in parts)), heads)
        tail[...] = fold3(jnp.exp(sum(dot_nt(after, p) for p in parts)), heads)
        write_t[...] = left3(write_ref[...].T)
        read_t[...] = left3(read_ref[...].T)

    first = step * (lanes // width)
    spread = spread_matrix(packed.shape[0], lanes, first, heads, width)
    slot = slot_ref[0]
    for which, (value_ref, weight, factor) in enumerate(
        ((x_ref, tail, write_t), (g_ref, lead, read_t))
    ):
        scale = dot(weight[...], spread)
        stage[which] = dot3(factor[...], *split(value_ref[...] * scale))
        if which == 1:
            decay_out[...] = jnp.broadcast_to(scale[rows - 1 :], decay_out.shape)
    begin = 0
    for k, blocks in enumerate(groups):

        @pl.when(jnp.logical_and(step >= begin, step < begin + blocks))
        def _(k=k):
            for which in range(2):
                for relative in range(4):
                    start = pl.multiple_of((slot ^ relative) * quarter, quarter)
                    target = out_refs[2 * k + relative // 2]
                    target[which, relative % 2] = stage[which, pl.ds(start, quarter), :]

        begin += blocks


def prepare_kernel(
    gain_ref, _late, decay_ref, write_ref, read_ref, left_y, left_x, left_c, left_b, up, down, edges,
    skip_ref, packed
):
    heads, rows = decay_ref.shape
    middle = CHUNK // 2 - 1
    columns = skip_ref.shape[1]
    gains = jnp.broadcast_to(gain_ref[...], (16, heads))
    head, lane = iota((heads, columns), 0), iota((heads, columns), 1)
    start = head * (columns // heads)
    hit = jnp.logical_and(lane >= start, lane < start + columns // heads)
    spread = jnp.where(hit, 1.0, 0.0).astype(BF16)
    skip_ref[...] = sum(dot(p, spread) for p in split3(gains))[:1]
    pack_decay(packed, decay_ref, heads)
    t, u = iota((CHUNK, CHUNK), 0), iota((CHUNK, CHUNK), 1)
    ahead = jnp.logical_and(u > middle, u <= t)
    behind = jnp.logical_and(u <= middle, u > t)
    signed = jnp.where(ahead, 1.0, jnp.where(behind, -1.0, 0.0)).astype(BF16)
    row, column = iota((16, CHUNK), 0), iota((16, CHUNK), 1)
    half = jnp.where((row == 0) == (column <= middle), 1.0, 0.0).astype(BF16)
    for i in range(rows // CHUNK):
        span = slice(i * CHUNK, (i + 1) * CHUNK)
        parts = split3(packed[:, span])
        gap = sum(dot_nt(signed, p) for p in parts)
        up[span, :] = fold3(jnp.exp(gap), heads)
        down[span, :] = fold3(jnp.exp(-gap), heads)
        edges[i] = fold3(jnp.exp(sum(dot_nt(half, p) for p in parts)), heads)
        write, read = write_ref[span, :], read_ref[span, :]
        write_p, read_p = split(write), split(read)
        scores = jnp.where(u <= t, three(dot_nt, read_p, write_p), 0.0)
        left_y[i] = left3(jnp.concatenate([scores, write.T], 0))
        scores = jnp.where(u >= t, three(dot_nt, write_p, read_p), 0.0)
        left_x[i] = left3(jnp.concatenate([scores, read.T], 0))
        left_c[i] = left3(read)
        left_b[i] = left3(write)


def fold_pair(a, b, size):
    lower = iota(a.shape, 1) % (2 * size) < size
    return jnp.where(
        lower, a + pltpu.roll(a, PACK - size, 1), b + pltpu.roll(b, size, 1)
    )


def fold_heads(x):
    tiles = [x[:, k * PACK : (k + 1) * PACK] for k in range(4)]
    return fold_pair(fold_pair(tiles[0], tiles[1], 32), fold_pair(tiles[2], tiles[3], 32), 16)


def gather_matrix(first):
    lane, column = iota((2 * PACK, PACK), 0) % PACK, iota((2 * PACK, PACK), 1)
    head = lane % 32 // 16 * 4 + lane % 64 // 32 * 2 + lane // 64
    return jnp.where(column == first + head, 1.0, 0.0).astype(BF16)


def block_kernel(
    slot_ref, left_y, left_x, left_c, left_b, up, down, edges, write_ref, read_ref, skip_ref,
    x_ref, g_ref, mine_ref, other_ref, *refs, first_head, heads, width, chained, closing
):
    if chained:
        _, _, old_read, old_write, old_sums, *refs = refs
    y_ref, dx_ref, acc_read, acc_write, sums, *refs = refs
    if closing:
        gd_ref, gw_ref, gr_ref, *refs = refs
    (
        state_in, grad_in, ups, downs, right_h, right_l, held, inner, folded, turned_h, turned_l,
        ends, outer
    ) = refs
    step, last = pl.program_id(0), pl.num_programs(0) - 1
    rows, lanes = x_ref.shape
    state = state_in.shape[0]
    quarter = state // 4
    count = rows // CHUNK
    span = [slice(i * CHUNK, (i + 1) * CHUNK) for i in range(count)]

    @pl.when(step == 0)
    def _():
        acc_read[...] = old_read[...] if chained else jnp.zeros_like(acc_read)
        acc_write[...] = old_write[...] if chained else jnp.zeros_like(acc_write)
        sums[...] = old_sums[...] if chained else jnp.zeros_like(sums)

    first = first_head + step * (lanes // width)
    spread = spread_matrix(PACK, lanes, first, heads, width)
    edge = [dot(edges[i], spread) for i in range(count)]
    skip = skip_ref[...]
    ups[...] = dot(up[...], spread)
    downs[...] = dot(down[...], spread)
    slot = slot_ref[0]
    for relative in range(4):
        start = pl.multiple_of((slot ^ relative) * quarter, quarter)
        source = mine_ref if relative < 2 else other_ref
        state_in[pl.ds(start, quarter), :] = source[0, relative % 2]
        grad_in[pl.ds(start, quarter), :] = source[1, relative % 2]

    ahead = edge[0][0:1] * state_in[...]
    back = edge[count - 1][1:2] * grad_in[...]
    for i in range(count):
        x, g = x_ref[span[i], :], g_ref[span[i], :]
        xh, xl = split(x * downs[span[i], :])
        ph, pl_ = split(ahead)
        right_h[i, :CHUNK], right_l[i, :CHUNK] = xh, xl
        right_h[i, CHUNK:], right_l[i, CHUNK:] = ph, pl_
        both = dot3(left_y[i], xh, xl)
        made = (both[:CHUNK] + dot3(left_c[i], ph, pl_)) * ups[span[i], :]
        y_ref[span[i], :] = made + skip * x
        inner[span[i], :] = made * g
        total = ahead + both[CHUNK:]
        held[i] = total
        if i + 1 < count:
            ahead = edge[i + 1][0:1] * (edge[i][1:2] * total)

        j = count - 1 - i
        x, g = x_ref[span[j], :], g_ref[span[j], :]
        gh, gl = split(g * ups[span[j], :])
        qh, ql = split(back)
        turned_h[j, :CHUNK], turned_l[j, :CHUNK] = gh, gl
        turned_h[j, CHUNK:], turned_l[j, CHUNK:] = qh, ql
        both = dot3(left_x[j] if j > 0 else left_x[j, :CHUNK], gh, gl)
        made = (both[:CHUNK] + dot3(left_b[j], qh, ql)) * downs[span[j], :]
        dx_ref[span[j], :] = made + skip * g
        outer[span[j], :] = x * made
        ends[j] = back
        if j > 0:
            back = edge[j - 1][1:2] * (edge[j][0:1] * (back + both[CHUNK:]))

    bottom = iota((CHUNK, 1), 0) == CHUNK - 1
    for i in range(count):
        flow = jnp.sum(held[i] * ends[i], axis=0, keepdims=True)
        change = inner[span[i], :] - outer[span[i], :] + jnp.where(bottom, flow, 0.0)
        folded[span[i], :] = fold_heads(change)
        pairs = dot3_nt((right_h[i], right_l[i]), turned_h[i], turned_l[i])
        acc_read[i] += pairs[:, :CHUNK]
        acc_write[i] += pairs[:CHUNK, CHUNK:]

    ch, cl = split(folded[...])
    sums[...] += dot(jnp.concatenate([ch, cl], 1), gather_matrix(first))

    if closing:

        @pl.when(step == last)
        def _():
            s, t = iota((CHUNK, CHUNK), 0), iota((CHUNK, CHUNK), 1)
            until = jnp.where(s >= t, 1.0, 0.0).astype(BF16)
            for i in range(count):
                scores = jnp.where(s <= t, acc_read[i, :CHUNK], 0.0)
                write, read = split(write_ref[span[i], :]), split(read_ref[span[i], :])
                gr_ref[span[i], :] = acc_read[i, CHUNK:].T + three(dot, split(scores.T), write)
                gw_ref[span[i], :] = acc_write[i] + three(dot, split(scores), read)
                parts = split3(sums[span[i], :].T)
                gd_ref[:, span[i]] = sum(dot(p, until) for p in parts)[:heads]


def whole(shape):
    return pl.BlockSpec(shape, lambda *_: (0,) * len(shape))


def make_states(slot, log_decay, state_write, state_read, inputs, grad_output, groups):
    rows, columns = inputs.shape
    heads, state = log_decay.shape[0], state_write.shape[1]
    quarter = state // 4
    wide = pl.BlockSpec((rows, LANES), lambda j, _: (0, j))
    shapes, specs, begin = [], [], 0
    for count in groups:
        shape = jax.ShapeDtypeStruct((2, 2, quarter, count * LANES), F32)
        spec = pl.BlockSpec(
            (2, 2, quarter, LANES),
            lambda j, _, begin=begin, count=count: (0, 0, 0, jnp.clip(j - begin, 0, count - 1)),
        )
        shapes += [shape, shape]
        specs += [spec, spec]
        begin += count
    blocks = begin
    width = columns // heads
    return pl.pallas_call(
        functools.partial(state_kernel, groups=groups, heads=heads, width=width),
        out_shape=(*shapes, jax.ShapeDtypeStruct((8, columns), F32)),
        grid_spec=pltpu.PrefetchScalarGridSpec(
            num_scalar_prefetch=1,
            grid=(blocks,),
            in_specs=[
                whole((heads, rows)), whole((rows, state)), whole((rows, state)), wide, wide
            ],
            out_specs=(*specs, pl.BlockSpec((8, LANES), lambda j, _: (0, j))),
            scratch_shapes=[
                pltpu.VMEM((PACK, rows), F32),
                pltpu.VMEM((rows, PACK), BF16),
                pltpu.VMEM((rows, PACK), BF16),
                pltpu.VMEM((state, 3 * rows), BF16),
                pltpu.VMEM((state, 3 * rows), BF16),
                pltpu.VMEM((2, state, LANES), F32),
            ],
        ),
        compiler_params=pltpu.CompilerParams(vmem_limit_bytes=VMEM),
        cost_estimate=pl.CostEstimate(
            flops=12 * rows * state * blocks * LANES,
            bytes_accessed=8 * rows * blocks * LANES,
            transcendentals=0,
        ),
    )(slot, log_decay, state_write, state_read, inputs, grad_output)


def prepare(log_decay, state_write, state_read, gains, late, columns):
    heads, rows = log_decay.shape
    state = state_write.shape[1]
    count = rows // CHUNK
    left = jax.ShapeDtypeStruct((count, CHUNK + state, 3 * CHUNK), BF16)
    side = jax.ShapeDtypeStruct((count, CHUNK, 3 * state), BF16)
    column = jax.ShapeDtypeStruct((rows, PACK), BF16)
    edges = jax.ShapeDtypeStruct((count, 16, PACK), BF16)
    small = [whole((heads, rows)), whole((rows, state)), whole((rows, state))]
    return pl.pallas_call(
        prepare_kernel,
        in_specs=[whole((1, heads)), ANYWHERE, *small],
        out_shape=(
            left, left, side, side, column, column, edges, jax.ShapeDtypeStruct((1, columns), F32)
        ),
        scratch_shapes=[pltpu.VMEM((PACK, rows), F32)],
        cost_estimate=pl.CostEstimate(flops=1 << 30, bytes_accessed=6 << 20, transcendentals=0),
    )(gains, late, log_decay, state_write, state_read)


def make_outputs(
    slot, prepared, skip, inputs, grad_output, pieces, heads, first, blocks, earlier, closing
):
    rows, columns = inputs.shape
    state = prepared[7].shape[1]
    quarter, count = state // 4, rows // CHUNK
    width = columns // heads
    wide = pl.BlockSpec((rows, LANES), lambda j, _: (0, first + j))
    part = pl.BlockSpec((2, 2, quarter, LANES), lambda j, _: (0, 0, 0, j))
    line = pl.BlockSpec((1, LANES), lambda j, _: (0, first + j))
    totals = [(count, CHUNK + state, CHUNK), (count, CHUNK, state), (rows, PACK)]
    in_specs = [*(whole(a.shape) for a in prepared), line, wide, wide, part, part]
    operands = [*prepared, skip, inputs, grad_output, *pieces]
    aliases = {}
    if earlier is not None:
        aliases = {len(operands) + 1: 0, len(operands) + 2: 1}
        in_specs += [ANYWHERE] * 2 + [whole(s) for s in totals]
        operands += earlier
    shapes = [(rows, columns)] * 2 + totals
    out_specs = [wide, wide, *(whole(s) for s in totals)]
    if closing:
        sides = [(heads, rows), (rows, state), (rows, state)]
        shapes += sides
        out_specs += [whole(s) for s in sides]
    return pl.pallas_call(
        functools.partial(
            block_kernel,
            first_head=first * LANES // width,
            heads=heads,
            width=width,
            chained=earlier is not None,
            closing=closing,
        ),
        out_shape=tuple(jax.ShapeDtypeStruct(s, F32) for s in shapes),
        grid_spec=pltpu.PrefetchScalarGridSpec(
            num_scalar_prefetch=1,
            grid=(blocks,),
            in_specs=in_specs,
            out_specs=tuple(out_specs),
            scratch_shapes=[
                pltpu.VMEM((state, LANES), F32),
                pltpu.VMEM((state, LANES), F32),
                pltpu.VMEM((rows, LANES), F32),
                pltpu.VMEM((rows, LANES), F32),
                pltpu.VMEM((count, CHUNK + state, LANES), BF16),
                pltpu.VMEM((count, CHUNK + state, LANES), BF16),
                pltpu.VMEM((count, state, LANES), F32),
                pltpu.VMEM((rows, LANES), F32),
                pltpu.VMEM((rows, PACK), F32),
                pltpu.VMEM((count, CHUNK + state, LANES), BF16),
                pltpu.VMEM((count, CHUNK + state, LANES), BF16),
                pltpu.VMEM((count, state, LANES), F32),
                pltpu.VMEM((rows, LANES), F32),
            ],
        ),
        input_output_aliases=aliases,
        compiler_params=pltpu.CompilerParams(vmem_limit_bytes=32 << 20),
        cost_estimate=pl.CostEstimate(
            flops=140 * rows * state * blocks * LANES,
            bytes_accessed=16 * rows * blocks * LANES,
            transcendentals=0,
        ),
    )(slot, *operands)


def local(inputs, log_decay, state_write, state_read, skip_gain, grad_output):
    hbm = functools.partial(pltpu.with_memory_space_constraint, memory_space=pltpu.HBM)
    inputs, grad_output = hbm(inputs), hbm(grad_output)
    state_write, state_read, log_decay = hbm(state_write), hbm(state_read), hbm(log_decay)
    heads = log_decay.shape[0]
    rows, columns = inputs.shape
    width = columns // heads
    devices, position = lax.axis_size("seq"), lax.axis_index("seq")
    planes = devices // 4
    core, chip, plane = position % 2, (position // 2) % 2, position // 4
    slot = (core * 2 + chip).astype(jnp.int32).reshape(1)
    swap_core = [(i, i ^ 1) for i in range(devices)]
    swap_chip = [(i, i ^ 2) for i in range(devices)]

    is_c0, is_y0 = core == 0, chip == 0
    goings = []
    made = make_states(slot, log_decay, state_write, state_read, inputs, grad_output, GROUPS)
    own = made[-1][0]
    twin, beside, across = (
        lax.ppermute(own, "seq", [(i, i ^ bits) for i in range(devices)]) for bits in (1, 2, 3)
    )
    here, there = own * twin, beside * across
    one = jnp.ones((columns,), F32)

    def travel(first, blocks, keep, send):
        lanes = slice(first * LANES, (first + blocks) * LANES)
        c0 = jnp.where(is_c0, own, twin)[lanes]
        c1 = jnp.where(is_c0, twin, own)[lanes]
        y0 = jnp.where(is_y0, here, there)[lanes]
        y1 = jnp.where(is_y0, there, here)[lanes]
        whole_plane = (here * there)[lanes]
        ones = one[lanes]
        near_core = lax.ppermute(send, "seq", swap_core)
        chip_f = jnp.where(is_c0, c1, ones) * keep[0] + jnp.where(is_c0, ones, c1) * near_core[0]
        chip_b = jnp.where(is_c0, ones, c0) * keep[1] + jnp.where(is_c0, c0, ones) * near_core[1]
        going = jnp.stack([chip_f[1], chip_b[1]])
        near_chip = lax.ppermute(going, "seq", swap_chip)
        if not goings:
            goings.append(prepare(
                    log_decay, state_write, state_read, skip_gain.reshape(1, heads), going, columns
                ))
            near_chip, _ = lax.optimization_barrier((near_chip, goings[0][-1]))
        plane_f = jnp.where(is_y0, y1, ones) * chip_f[0] + jnp.where(is_y0, ones, y1) * near_chip[0]
        plane_b = jnp.where(is_y0, ones, y0) * chip_b[0] + jnp.where(is_y0, y0, ones) * near_chip[1]
        ahead = jnp.zeros_like(plane_f)
        back = jnp.zeros_like(plane_b)
        for hop in range(planes - 1):
            mirror = planes - 1 - hop
            going = jnp.where(
                plane == hop, whole_plane * ahead + plane_f, whole_plane * back + plane_b
            )
            pairs = [
                (source * 4 + i, target * 4 + i)
                for source, target in ((hop, hop + 1), (mirror, mirror - 1))
                for i in range(4)
            ]
            came = lax.ppermute(going, "seq", pairs)
            ahead = jnp.where(plane == hop + 1, came, ahead)
            back = jnp.where(plane == mirror - 1, came, back)
        mine = jnp.stack(
            [
                jnp.where(is_y0, ahead, y0 * ahead + near_chip[0]),
                jnp.where(is_y0, y1 * back + near_chip[1], back),
            ]
        )
        theirs = jnp.stack(
            [
                jnp.where(is_y0, y0 * ahead + chip_f[0], ahead),
                jnp.where(is_y0, back, y1 * back + chip_b[0]),
            ]
        )
        came = lax.ppermute(theirs, "seq", swap_chip)
        into_f = jnp.stack([mine[0], came[0]])
        into_b = jnp.stack([mine[1], came[1]])
        mine = jnp.stack(
            [
                jnp.where(is_c0, into_f, c0 * into_f + near_core[0]),
                jnp.where(is_c0, c1 * into_b + near_core[1], into_b),
            ]
        )
        theirs = jnp.stack(
            [
                jnp.where(is_c0, c0 * into_f + keep[0], into_f),
                jnp.where(is_c0, into_b, c1 * into_b + keep[1]),
            ]
        )
        return mine, lax.ppermute(theirs, "seq", swap_core)

    travels = []
    first = 0
    for k, blocks in enumerate(GROUPS):
        pair = made[2 * k : 2 * k + 2]
        travels.append((first, blocks, travel(first, blocks, *pair)))
        first += blocks
    *prepared, skip = goings[0]
    prepared += [state_write, state_read]
    results = None
    for k, (first, blocks, pieces) in enumerate(travels):
        results = make_outputs(
            slot, prepared, skip, inputs, grad_output, pieces, heads, first, blocks, results,
            k + 1 == len(travels)
        )
    outputs, grad_inputs, _, _, _, grad_decay, grad_write, grad_read = results
    return (outputs, grad_inputs, grad_decay, grad_write, grad_read)


def solution(mesh):
    in_specs = (
        P(("group", "seq"), None),
        P(None, ("group", "seq")),
        P(("group", "seq"), None),
        P(("group", "seq"), None),
        P(),
        P(("group", "seq"), None),
    )
    out_specs = (
        P(("group", "seq"), None),
        P(("group", "seq"), None),
        P(None, ("group", "seq")),
        P(("group", "seq"), None),
        P(("group", "seq"), None),
    )
    return jax.shard_map(local, mesh=mesh, in_specs=in_specs, out_specs=out_specs, check_vma=False)
```

```python
import functools
import math

import jax
import jax.numpy as jnp
from jax import lax
from jax.experimental import pallas as pl
from jax.experimental.pallas import tpu as pltpu
from jax.sharding import PartitionSpec as P

CHUNK = 128
LANES = 512
PACK = 128
GROUPS = (3, 2)
VMEM = 24 << 20
ANYWHERE = pl.BlockSpec(memory_space=pl.ANY)
F32 = jnp.float32
BF16 = jnp.bfloat16


def dot(a, b):
    return lax.dot_general(a, b, (((1,), (0,)), ((), ())), preferred_element_type=F32)


def dot_nt(a, b):
    return lax.dot_general(a, b, (((1,), (1,)), ((), ())), preferred_element_type=F32)


def split(x):
    high = x.astype(BF16)
    return high, (x - high.astype(F32)).astype(BF16)


def split3(x):
    high = x.astype(BF16)
    rest = x - high.astype(F32)
    middle = rest.astype(BF16)
    return high, middle, (rest - middle.astype(F32)).astype(BF16)


def three(product, a, b):
    return product(a[0], b[0]) + product(a[0], b[1]) + product(a[1], b[0])


def left3(x):
    high, low = split(x)
    return jnp.concatenate([high, high, low], 1)


def dot3(left, high, low):
    depth = left.shape[1] // 3
    a, b = left[:, :depth], left[:, 2 * depth :]
    rows = left.shape[0]
    both = dot(
        jnp.concatenate([jnp.concatenate([a, a], 1), jnp.concatenate([b, b], 1)], 0),
        jnp.concatenate([high, low], 0),
    )
    return both[:rows] + both[rows:]


def dot3_nt(a, high, low):
    rows = a[0].shape[0]
    both = dot_nt(jnp.concatenate([a[0], a[1]], 0), high)
    return both[:rows] + both[rows:] + dot_nt(a[0], low)


def iota(shape, axis):
    return lax.broadcasted_iota(jnp.int32, shape, axis)


def fold3(x, heads):
    high, middle, low = split3(x)
    column = iota(x.shape, 1)
    chosen = jnp.where(
        column < heads,
        high.astype(F32),
        jnp.where(column < 2 * heads, middle.astype(F32), low.astype(F32)),
    )
    return chosen.astype(BF16)


def spread_matrix(rows, lanes, first, heads, width):
    row, lane = iota((rows, lanes), 0), iota((rows, lanes), 1)
    hit = None
    for copy in range(3):
        start = (row - (first + copy * heads)) * width
        one = jnp.logical_and(lane >= start, lane < start + width)
        hit = one if hit is None else jnp.logical_or(hit, one)
    return jnp.where(hit, 1.0, 0.0).astype(BF16)


def pack_decay(packed, decay_ref, heads):
    packed[...] = jnp.zeros_like(packed)
    for copy in range(3):
        packed[copy * heads : (copy + 1) * heads, :] = decay_ref[...]


def state_kernel(
    slot_ref, decay_ref, write_ref, read_ref, x_ref, g_ref, *refs, groups, heads, width
):
    *out_refs, decay_out, packed, tail, lead, write_t, read_t, stage = refs
    step = pl.program_id(0)
    rows, lanes = x_ref.shape
    state = write_ref.shape[1]
    quarter = state // 4

    @pl.when(step == 0)
    def _():
        pack_decay(packed, decay_ref, heads)
        parts = split3(packed[...])
        t, u = iota((rows, rows), 0), iota((rows, rows), 1)
        before = jnp.where(u <= t, 1.0, 0.0).astype(BF16)
        after = jnp.where(u > t, 1.0, 0.0).astype(BF16)
        lead[...] = fold3(jnp.exp(sum(dot_nt(before, p) for p in parts)), heads)
        tail[...] = fold3(jnp.exp(sum(dot_nt(after, p) for p in parts)), heads)
        write_t[...] = left3(write_ref[...].T)
        read_t[...] = left3(read_ref[...].T)

    first = step * (lanes // width)
    spread = spread_matrix(packed.shape[0], lanes, first, heads, width)
    slot = slot_ref[0]
    for which, (value_ref, weight, factor) in enumerate(
        ((x_ref, tail, write_t), (g_ref, lead, read_t))
    ):
        scale = dot(weight[...], spread)
        high, low = split(value_ref[...] * scale)
        half = rows // 2
        stage[which] = sum(
            dot(factor[:, k * rows + h * half : k * rows + (h + 1) * half], part[h * half : (h + 1) * half])
            for h in range(2)
            for k, part in ((0, high), (1, low), (2, high))
        )
        if which == 1:
            decay_out[...] = jnp.broadcast_to(scale[rows - 1 :], decay_out.shape)
    begin = 0
    for k, blocks in enumerate(groups):

        @pl.when(jnp.logical_and(step >= begin, step < begin + blocks))
        def _(k=k):
            for which in range(2):
                for relative in range(4):
                    start = pl.multiple_of((slot ^ relative) * quarter, quarter)
                    target = out_refs[2 * k + relative // 2]
                    target[which, relative % 2] = stage[which, pl.ds(start, quarter), :]

        begin += blocks


def prepare_kernel(
    gain_ref, _late, decay_ref, write_ref, read_ref, left_y, left_x, left_c, left_b, up, down, edges,
    skip_ref, packed
):
    heads, rows = decay_ref.shape
    middle = CHUNK // 2 - 1
    columns = skip_ref.shape[1]
    gains = jnp.broadcast_to(gain_ref[...], (16, heads))
    head, lane = iota((heads, columns), 0), iota((heads, columns), 1)
    start = head * (columns // heads)
    hit = jnp.logical_and(lane >= start, lane < start + columns // heads)
    spread = jnp.where(hit, 1.0, 0.0).astype(BF16)
    skip_ref[...] = sum(dot(p, spread) for p in split3(gains))[:1]
    pack_decay(packed, decay_ref, heads)
    t, u = iota((CHUNK, CHUNK), 0), iota((CHUNK, CHUNK), 1)
    ahead = jnp.logical_and(u > middle, u <= t)
    behind = jnp.logical_and(u <= middle, u > t)
    signed = jnp.where(ahead, 1.0, jnp.where(behind, -1.0, 0.0)).astype(BF16)
    row, column = iota((16, CHUNK), 0), iota((16, CHUNK), 1)
    half = jnp.where((row == 0) == (column <= middle), 1.0, 0.0).astype(BF16)
    for i in range(rows // CHUNK):
        span = slice(i * CHUNK, (i + 1) * CHUNK)
        parts = split3(packed[:, span])
        gap = sum(dot_nt(signed, p) for p in parts)
        up[span, :] = fold3(jnp.exp(gap), heads)
        down[span, :] = fold3(jnp.exp(-gap), heads)
        edges[i] = fold3(jnp.exp(sum(dot_nt(half, p) for p in parts)), heads)
        write, read = write_ref[span, :], read_ref[span, :]
        write_p, read_p = split(write), split(read)
        scores = jnp.where(u <= t, three(dot_nt, read_p, write_p), 0.0)
        left_y[i] = left3(jnp.concatenate([scores, write.T], 0))
        scores = jnp.where(u >= t, three(dot_nt, write_p, read_p), 0.0)
        left_x[i] = left3(jnp.concatenate([scores, read.T], 0))
        left_c[i] = left3(read)
        left_b[i] = left3(write)


def fold_pair(a, b, size):
    lower = iota(a.shape, 1) % (2 * size) < size
    return jnp.where(
        lower, a + pltpu.roll(a, PACK - size, 1), b + pltpu.roll(b, size, 1)
    )


def fold_heads(x):
    tiles = [x[:, k * PACK : (k + 1) * PACK] for k in range(4)]
    return fold_pair(fold_pair(tiles[0], tiles[1], 32), fold_pair(tiles[2], tiles[3], 32), 16)


def gather_matrix(first):
    lane, column = iota((2 * PACK, PACK), 0) % PACK, iota((2 * PACK, PACK), 1)
    head = lane % 32 // 16 * 4 + lane % 64 // 32 * 2 + lane // 64
    return jnp.where(column == first + head, 1.0, 0.0).astype(BF16)


def block_kernel(
    slot_ref, left_y, left_x, left_c, left_b, up, down, edges, write_ref, read_ref, skip_ref,
    x_ref, g_ref, mine_ref, other_ref, *refs, first_head, heads, width, chained, closing
):
    if chained:
        _, _, old_read, old_write, old_sums, *refs = refs
    y_ref, dx_ref, acc_read, acc_write, sums, *refs = refs
    if closing:
        gd_ref, gw_ref, gr_ref, *refs = refs
    (
        state_in, grad_in, ups, downs, right_h, right_l, held, inner, folded, turned_h, turned_l,
        ends, outer
    ) = refs
    step, last = pl.program_id(0), pl.num_programs(0) - 1
    rows, lanes = x_ref.shape
    state = state_in.shape[0]
    quarter = state // 4
    count = rows // CHUNK
    span = [slice(i * CHUNK, (i + 1) * CHUNK) for i in range(count)]

    @pl.when(step == 0)
    def _():
        acc_read[...] = old_read[...] if chained else jnp.zeros_like(acc_read)
        acc_write[...] = old_write[...] if chained else jnp.zeros_like(acc_write)
        sums[...] = old_sums[...] if chained else jnp.zeros_like(sums)

    first = first_head + step * (lanes // width)
    spread = spread_matrix(PACK, lanes, first, heads, width)
    edge = [dot(edges[i], spread) for i in range(count)]
    skip = skip_ref[...]
    ups[...] = dot(up[...], spread)
    downs[...] = dot(down[...], spread)
    slot = slot_ref[0]
    for relative in range(4):
        start = pl.multiple_of((slot ^ relative) * quarter, quarter)
        source = mine_ref if relative < 2 else other_ref
        state_in[pl.ds(start, quarter), :] = source[0, relative % 2]
        grad_in[pl.ds(start, quarter), :] = source[1, relative % 2]

    ahead = edge[0][0:1] * state_in[...]
    back = edge[count - 1][1:2] * grad_in[...]
    for i in range(count):
        x, g = x_ref[span[i], :], g_ref[span[i], :]
        xh, xl = split(x * downs[span[i], :])
        ph, pl_ = split(ahead)
        right_h[i, :CHUNK], right_l[i, :CHUNK] = xh, xl
        right_h[i, CHUNK:], right_l[i, CHUNK:] = ph, pl_
        both = dot3(left_y[i], xh, xl)
        made = (both[:CHUNK] + dot3(left_c[i], ph, pl_)) * ups[span[i], :]
        y_ref[span[i], :] = made + skip * x
        inner[span[i], :] = made * g
        total = ahead + both[CHUNK:]
        held[i] = total
        if i + 1 < count:
            ahead = edge[i + 1][0:1] * (edge[i][1:2] * total)

        j = count - 1 - i
        x, g = x_ref[span[j], :], g_ref[span[j], :]
        gh, gl = split(g * ups[span[j], :])
        qh, ql = split(back)
        turned_h[j, :CHUNK], turned_l[j, :CHUNK] = gh, gl
        turned_h[j, CHUNK:], turned_l[j, CHUNK:] = qh, ql
        both = dot3(left_x[j] if j > 0 else left_x[j, :CHUNK], gh, gl)
        made = (both[:CHUNK] + dot3(left_b[j], qh, ql)) * downs[span[j], :]
        dx_ref[span[j], :] = made + skip * g
        outer[span[j], :] = x * made
        ends[j] = back
        if j > 0:
            back = edge[j - 1][1:2] * (edge[j][0:1] * (back + both[CHUNK:]))

    bottom = iota((CHUNK, 1), 0) == CHUNK - 1
    for i in range(count):
        flow = jnp.sum(held[i] * ends[i], axis=0, keepdims=True)
        change = inner[span[i], :] - outer[span[i], :] + jnp.where(bottom, flow, 0.0)
        folded[span[i], :] = fold_heads(change)
        pairs = dot3_nt((right_h[i], right_l[i]), turned_h[i], turned_l[i])
        acc_read[i] += pairs[:, :CHUNK]
        acc_write[i] += pairs[:CHUNK, CHUNK:]

    ch, cl = split(folded[...])
    sums[...] += dot(jnp.concatenate([ch, cl], 1), gather_matrix(first))

    if closing:

        @pl.when(step == last)
        def _():
            s, t = iota((CHUNK, CHUNK), 0), iota((CHUNK, CHUNK), 1)
            until = jnp.where(s >= t, 1.0, 0.0).astype(BF16)
            for i in range(count):
                scores = jnp.where(s <= t, acc_read[i, :CHUNK], 0.0)
                write, read = split(write_ref[span[i], :]), split(read_ref[span[i], :])
                gr_ref[span[i], :] = acc_read[i, CHUNK:].T + three(dot, split(scores.T), write)
                gw_ref[span[i], :] = acc_write[i] + three(dot, split(scores), read)
                parts = split3(sums[span[i], :].T)
                gd_ref[:, span[i]] = sum(dot(p, until) for p in parts)[:heads]


def whole(shape):
    return pl.BlockSpec(shape, lambda *_: (0,) * len(shape))


def make_states(slot, log_decay, state_write, state_read, inputs, grad_output, groups):
    rows, columns = inputs.shape
    heads, state = log_decay.shape[0], state_write.shape[1]
    quarter = state // 4
    wide = pl.BlockSpec((rows, LANES), lambda j, _: (0, j))
    shapes, specs, begin = [], [], 0
    for count in groups:
        shape = jax.ShapeDtypeStruct((2, 2, quarter, count * LANES), F32)
        spec = pl.BlockSpec(
            (2, 2, quarter, LANES),
            lambda j, _, begin=begin, count=count: (0, 0, 0, jnp.clip(j - begin, 0, count - 1)),
        )
        shapes += [shape, shape]
        specs += [spec, spec]
        begin += count
    blocks = begin
    width = columns // heads
    return pl.pallas_call(
        functools.partial(state_kernel, groups=groups, heads=heads, width=width),
        out_shape=(*shapes, jax.ShapeDtypeStruct((8, columns), F32)),
        grid_spec=pltpu.PrefetchScalarGridSpec(
            num_scalar_prefetch=1,
            grid=(blocks,),
            in_specs=[
                whole((heads, rows)), whole((rows, state)), whole((rows, state)), wide, wide
            ],
            out_specs=(*specs, pl.BlockSpec((8, LANES), lambda j, _: (0, j))),
            scratch_shapes=[
                pltpu.VMEM((PACK, rows), F32),
                pltpu.VMEM((rows, PACK), BF16),
                pltpu.VMEM((rows, PACK), BF16),
                pltpu.VMEM((state, 3 * rows), BF16),
                pltpu.VMEM((state, 3 * rows), BF16),
                pltpu.VMEM((2, state, LANES), F32),
            ],
        ),
        compiler_params=pltpu.CompilerParams(vmem_limit_bytes=VMEM),
        cost_estimate=pl.CostEstimate(
            flops=12 * rows * state * blocks * LANES,
            bytes_accessed=8 * rows * blocks * LANES,
            transcendentals=0,
        ),
    )(slot, log_decay, state_write, state_read, inputs, grad_output)


def prepare(log_decay, state_write, state_read, gains, late, columns):
    heads, rows = log_decay.shape
    state = state_write.shape[1]
    count = rows // CHUNK
    left = jax.ShapeDtypeStruct((count, CHUNK + state, 3 * CHUNK), BF16)
    side = jax.ShapeDtypeStruct((count, CHUNK, 3 * state), BF16)
    column = jax.ShapeDtypeStruct((rows, PACK), BF16)
    edges = jax.ShapeDtypeStruct((count, 16, PACK), BF16)
    small = [whole((heads, rows)), whole((rows, state)), whole((rows, state))]
    return pl.pallas_call(
        prepare_kernel,
        in_specs=[whole((1, heads)), ANYWHERE, *small],
        out_shape=(
            left, left, side, side, column, column, edges, jax.ShapeDtypeStruct((1, columns), F32)
        ),
        scratch_shapes=[pltpu.VMEM((PACK, rows), F32)],
        cost_estimate=pl.CostEstimate(flops=1 << 30, bytes_accessed=6 << 20, transcendentals=0),
    )(gains, late, log_decay, state_write, state_read)


def make_outputs(
    slot, prepared, skip, inputs, grad_output, pieces, heads, first, blocks, earlier, closing
):
    rows, columns = inputs.shape
    state = prepared[7].shape[1]
    quarter, count = state // 4, rows // CHUNK
    width = columns // heads
    wide = pl.BlockSpec((rows, LANES), lambda j, _: (0, first + j))
    part = pl.BlockSpec((2, 2, quarter, LANES), lambda j, _: (0, 0, 0, j))
    line = pl.BlockSpec((1, LANES), lambda j, _: (0, first + j))
    totals = [(count, CHUNK + state, CHUNK), (count, CHUNK, state), (rows, PACK)]
    in_specs = [*(whole(a.shape) for a in prepared), line, wide, wide, part, part]
    operands = [*prepared, skip, inputs, grad_output, *pieces]
    aliases = {}
    if earlier is not None:
        aliases = {len(operands) + 1: 0, len(operands) + 2: 1}
        in_specs += [ANYWHERE] * 2 + [whole(s) for s in totals]
        operands += earlier
    shapes = [(rows, columns)] * 2 + totals
    out_specs = [wide, wide, *(whole(s) for s in totals)]
    if closing:
        sides = [(heads, rows), (rows, state), (rows, state)]
        shapes += sides
        out_specs += [whole(s) for s in sides]
    return pl.pallas_call(
        functools.partial(
            block_kernel,
            first_head=first * LANES // width,
            heads=heads,
            width=width,
            chained=earlier is not None,
            closing=closing,
        ),
        out_shape=tuple(jax.ShapeDtypeStruct(s, F32) for s in shapes),
        grid_spec=pltpu.PrefetchScalarGridSpec(
            num_scalar_prefetch=1,
            grid=(blocks,),
            in_specs=in_specs,
            out_specs=tuple(out_specs),
            scratch_shapes=[
                pltpu.VMEM((state, LANES), F32),
                pltpu.VMEM((state, LANES), F32),
                pltpu.VMEM((rows, LANES), F32),
                pltpu.VMEM((rows, LANES), F32),
                pltpu.VMEM((count, CHUNK + state, LANES), BF16),
                pltpu.VMEM((count, CHUNK + state, LANES), BF16),
                pltpu.VMEM((count, state, LANES), F32),
                pltpu.VMEM((rows, LANES), F32),
                pltpu.VMEM((rows, PACK), F32),
                pltpu.VMEM((count, CHUNK + state, LANES), BF16),
                pltpu.VMEM((count, CHUNK + state, LANES), BF16),
                pltpu.VMEM((count, state, LANES), F32),
                pltpu.VMEM((rows, LANES), F32),
            ],
        ),
        input_output_aliases=aliases,
        compiler_params=pltpu.CompilerParams(vmem_limit_bytes=32 << 20),
        cost_estimate=pl.CostEstimate(
            flops=140 * rows * state * blocks * LANES,
            bytes_accessed=16 * rows * blocks * LANES,
            transcendentals=0,
        ),
    )(slot, *operands)


def local(inputs, log_decay, state_write, state_read, skip_gain, grad_output):
    hbm = functools.partial(pltpu.with_memory_space_constraint, memory_space=pltpu.HBM)
    inputs, grad_output = hbm(inputs), hbm(grad_output)
    state_write, state_read, log_decay = hbm(state_write), hbm(state_read), hbm(log_decay)
    heads = log_decay.shape[0]
    rows, columns = inputs.shape
    width = columns // heads
    devices, position = lax.axis_size("seq"), lax.axis_index("seq")
    planes = devices // 4
    core, chip, plane = position % 2, (position // 2) % 2, position // 4
    slot = (core * 2 + chip).astype(jnp.int32).reshape(1)
    swap_core = [(i, i ^ 1) for i in range(devices)]
    swap_chip = [(i, i ^ 2) for i in range(devices)]

    is_c0, is_y0 = core == 0, chip == 0
    goings = []
    made = make_states(slot, log_decay, state_write, state_read, inputs, grad_output, GROUPS)
    own = made[-1][0]
    twin, beside, across = (
        lax.ppermute(own, "seq", [(i, i ^ bits) for i in range(devices)]) for bits in (1, 2, 3)
    )
    here, there = own * twin, beside * across
    one = jnp.ones((columns,), F32)

    def travel(first, blocks, keep, send):
        lanes = slice(first * LANES, (first + blocks) * LANES)
        c0 = jnp.where(is_c0, own, twin)[lanes]
        c1 = jnp.where(is_c0, twin, own)[lanes]
        y0 = jnp.where(is_y0, here, there)[lanes]
        y1 = jnp.where(is_y0, there, here)[lanes]
        whole_plane = (here * there)[lanes]
        ones = one[lanes]
        near_core = lax.ppermute(send, "seq", swap_core)
        chip_f = jnp.where(is_c0, c1, ones) * keep[0] + jnp.where(is_c0, ones, c1) * near_core[0]
        chip_b = jnp.where(is_c0, ones, c0) * keep[1] + jnp.where(is_c0, c0, ones) * near_core[1]
        going = jnp.stack([chip_f[1], chip_b[1]])
        near_chip = lax.ppermute(going, "seq", swap_chip)
        if not goings:
            goings.append(prepare(
                    log_decay, state_write, state_read, skip_gain.reshape(1, heads), going, columns
                ))
            near_chip, _ = lax.optimization_barrier((near_chip, goings[0][-1]))
        plane_f = jnp.where(is_y0, y1, ones) * chip_f[0] + jnp.where(is_y0, ones, y1) * near_chip[0]
        plane_b = jnp.where(is_y0, ones, y0) * chip_b[0] + jnp.where(is_y0, y0, ones) * near_chip[1]
        ahead = jnp.zeros_like(plane_f)
        back = jnp.zeros_like(plane_b)
        for hop in range(planes - 1):
            mirror = planes - 1 - hop
            going = jnp.where(
                plane == hop, whole_plane * ahead + plane_f, whole_plane * back + plane_b
            )
            pairs = [
                (source * 4 + i, target * 4 + i)
                for source, target in ((hop, hop + 1), (mirror, mirror - 1))
                for i in range(4)
            ]
            came = lax.ppermute(going, "seq", pairs)
            ahead = jnp.where(plane == hop + 1, came, ahead)
            back = jnp.where(plane == mirror - 1, came, back)
        mine = jnp.stack(
            [
                jnp.where(is_y0, ahead, y0 * ahead + near_chip[0]),
                jnp.where(is_y0, y1 * back + near_chip[1], back),
            ]
        )
        theirs = jnp.stack(
            [
                jnp.where(is_y0, y0 * ahead + chip_f[0], ahead),
                jnp.where(is_y0, back, y1 * back + chip_b[0]),
            ]
        )
        came = lax.ppermute(theirs, "seq", swap_chip)
        into_f = jnp.stack([mine[0], came[0]])
        into_b = jnp.stack([mine[1], came[1]])
        mine = jnp.stack(
            [
                jnp.where(is_c0, into_f, c0 * into_f + near_core[0]),
                jnp.where(is_c0, c1 * into_b + near_core[1], into_b),
            ]
        )
        theirs = jnp.stack(
            [
                jnp.where(is_c0, c0 * into_f + keep[0], into_f),
                jnp.where(is_c0, into_b, c1 * into_b + keep[1]),
            ]
        )
        return mine, lax.ppermute(theirs, "seq", swap_core)

    travels = []
    first = 0
    for k, blocks in enumerate(GROUPS):
        pair = made[2 * k : 2 * k + 2]
        travels.append((first, blocks, travel(first, blocks, *pair)))
        first += blocks
    *prepared, skip = goings[0]
    prepared += [state_write, state_read]
    results = None
    for k, (first, blocks, pieces) in enumerate(travels):
        results = make_outputs(
            slot, prepared, skip, inputs, grad_output, pieces, heads, first, blocks, results,
            k + 1 == len(travels)
        )
    outputs, grad_inputs, _, _, _, grad_decay, grad_write, grad_read = results
    return (outputs, grad_inputs, grad_decay, grad_write, grad_read)


def solution(mesh):
    in_specs = (
        P(("group", "seq"), None),
        P(None, ("group", "seq")),
        P(("group", "seq"), None),
        P(("group", "seq"), None),
        P(),
        P(("group", "seq"), None),
    )
    out_specs = (
        P(("group", "seq"), None),
        P(("group", "seq"), None),
        P(None, ("group", "seq")),
        P(("group", "seq"), None),
        P(("group", "seq"), None),
    )
    return jax.shard_map(local, mesh=mesh, in_specs=in_specs, out_specs=out_specs, check_vma=False)
```
